768 devices in a mesh: blk: 48 (over z, y_lo), patch: 16 (over x, y_hi, core).
Axes of the slice: x: 4, y: 8 (y_hi: 2, y_lo: 4; y = y_hi * 4 + y_lo), z: 12, core: 2. Of those that a mesh axis runs over, the one named last changes fastest.
Arguments:
- queries: bfloat16 [24576, 8192], P('blk', 'patch'), may hold values from -6 to 6
- keys: bfloat16 [6144, 1024], P('blk'), may hold values from -6 to 6
- values: bfloat16 [6144, 1024], P('blk'), may hold values from -6 to 6
- outputs: bfloat16 [24576, 8192], P('blk', 'patch'), may hold values from -6 to 6
- out_grad: bfloat16 [24576, 8192], P('blk', 'patch'), may hold values from -6 to 6
- lse: float32 [24576, 64], P('blk', 'patch'), may hold values from 5 to 7
- doc_ids: int32 [24576], P('blk'), may hold values from 0 to 5, never falling along the last dimension, each value on 1 to 12288 neighbouring positions
- image_docs: int32 [48], replicated, may hold values from 0 to 5
Outputs:
- query_grad: bfloat16 [24576, 8192], P('blk', 'patch')
- kv_grad: bfloat16 [6144, 2048], P(('blk', 'patch'))
The draws below stay inside these ranges and needn't reach their ends.
Inputs may be any that keep to these rules, and one draw needn't show every extreme that they name: `doc_ids`: documents are runs of consecutive tokens, numbered in order; one document holds exactly 12288 tokens. `image_docs`: the image rows of block b are rows b * 128 to (b + 1) * 128 - 1.
All inputs are finite; a program needn't handle non-finite values.
Results may differ from the reference program's by a relative error of at most 0.0049.
Values may be sent and summed in bfloat16 or wider, within the bound.
No kernel may reach another device: no remote copies, remote signals or barrier semaphores. Data moves between devices by JAX's collectives and lax.ppermute only.
A program may use at most 64 MiB of HBM per device.

```python
import math
import jax
import jax.numpy as jnp
import numpy as np
from jax import lax

HEADS = 64
KVH = 8
DH = 128
TOK_DEV = 512
BLOCK = 128
DOCS = 6
TOKENS = 24576
IMG_ROWS = 6144
IMG_BLOCKS = 48
N_BLK = 48


def touch_ends(entries, stream_key, least, largest):
    longest = entries.shape.index(max(entries.shape))
    spots = []
    for shift in (0, 1):
        where = [jax.random.randint(jax.random.fold_in(stream_key, axis), (), 0, length) for axis, length in enumerate(entries.shape)]
        where[longest] = (where[longest] + shift) % entries.shape[longest]
        spots.append(tuple(where))
    return entries.at[spots[0]].set(least).at[spots[1]].set(largest)


def shard_levels(rng, shape, cuts, smallest, top_value):
    def one(dim, blocks):
        draws = jax.random.uniform(jax.random.fold_in(jax.random.fold_in(rng, 6), dim), (blocks,), jnp.float32, smallest / len(cuts), top_value / len(cuts))
        return jnp.repeat(jnp.exp(draws), shape[dim] // blocks).reshape((-1,) + (1,) * (len(shape) - dim - 1))

    level = one(*cuts[0])
    for cut in cuts[1:]:
        level = level * one(*cut)
    return level


def profile(number_of, total, most, skew):
    portions = [(1 << 20) // math.isqrt(rank ** skew) + 1 for rank in range(2, number_of + 1)]
    spare, counts = total - most - (number_of - 1), [1] * (number_of - 1)
    while spare > 0:
        candidates = [i for i in range(number_of - 1) if counts[i] < most]
        whole, left = sum([portions[i] for i in candidates]), spare
        for i in candidates:
            extra = min(most - counts[i], max(1, left * portions[i] // whole), spare)
            counts[i] = counts[i] + extra
            spare = spare - extra
    return np.array([most] + counts)


def ragged_sizes(key, count, total, reach, lean):
    if count == 2:
        one = jax.random.randint(key, (), max(1, total - reach), min(reach, total - 1) + 1)
        return jnp.stack([one, total - one])
    sizes = jnp.asarray(profile(count, total, reach, lean), jnp.int32)
    couples = (count - 1) // 2
    giver, sink = sizes[1:1 + 2 * couples:2], sizes[2:2 + 2 * couples:2]
    slack = jnp.minimum(giver - 1, reach - sink)
    shifted = jax.random.randint(jax.random.fold_in(key, 1), (couples,), 0, 1 << 20) % (slack + 1)
    sizes = sizes.at[1:1 + 2 * couples:2].set(giver - shifted).at[2:2 + 2 * couples:2].set(sink + shifted)
    return sizes[jax.random.permutation(jax.random.fold_in(key, 2), count)]


def bell_draw(own_key, extent, spread, most, pieces=(), dtype=jnp.bfloat16):
    drawn = spread * jax.random.normal(own_key, extent, jnp.float32)
    if pieces:
        drawn = drawn * shard_levels(own_key, extent, pieces, -0.22, 0.18)
    return jnp.clip(drawn, -most, most).astype(dtype)


def setup_inputs(seed: int = 0) -> dict:
    key_of = jax.random.split(jax.random.key(seed), 9)
    queries = bell_draw(key_of[0], (TOKENS, HEADS * DH), 1.0, 6.0, ((0, 48), (1, 16)))
    keys = bell_draw(key_of[1], (IMG_ROWS, KVH * DH), 1.0, 6.0, ((0, 48),))
    values = bell_draw(key_of[2], (IMG_ROWS, KVH * DH), 1.0, 6.0, ((0, 48),))
    outputs = bell_draw(key_of[3], (TOKENS, HEADS * DH), 1.0, 6.0, ((0, 48), (1, 16)))
    out_grad = bell_draw(key_of[4], (TOKENS, HEADS * DH), 1.0, 6.0, ((0, 48), (1, 16)))
    lse = jnp.clip(5.0 + 2.0 * jax.random.uniform(key_of[5], (TOKENS, HEADS), jnp.float32) ** shard_levels(key_of[5], (TOKENS, HEADS), ((0, 48), (1, 16)), -0.2, 0.2), 5.0, 7.0)
    doc_ids = jnp.searchsorted(jnp.cumsum(ragged_sizes(key_of[6], DOCS, TOKENS, TOKENS // 2, 2)), jnp.arange(TOKENS), side="right").astype(jnp.int32)
    image_docs = touch_ends(jax.random.randint(key_of[7], (IMG_BLOCKS,), 0, DOCS), jax.random.fold_in(key_of[7], 1), 0, DOCS - 1).astype(jnp.int32)
    return {"queries": queries, "keys": keys, "values": values, "outputs": outputs, "out_grad": out_grad, "lse": lse, "doc_ids": doc_ids, "image_docs": image_docs}


def reference(queries, keys, values, outputs, out_grad, lse, doc_ids, image_docs):
    group = HEADS // KVH
    scaling = DH ** -0.5
    row_doc = jnp.repeat(image_docs, BLOCK)
    key_all = keys.astype(jnp.float32).reshape(IMG_ROWS, KVH, DH)
    value_all = values.astype(jnp.float32).reshape(IMG_ROWS, KVH, DH)
    query_blocks = queries.reshape(N_BLK, TOK_DEV, KVH, group, DH)
    grad_blocks = out_grad.reshape(N_BLK, TOK_DEV, KVH, group, DH)
    output_blocks = outputs.reshape(N_BLK, TOK_DEV, KVH, group, DH)
    stat_blocks = lse.reshape(N_BLK, TOK_DEV, KVH, group)
    doc_blocks = doc_ids.reshape(N_BLK, TOK_DEV)

    def block_step(carry, inputs):
        dkey_sum, dvalue_sum = carry
        query_blk, grad_blk, output_blk, stat_blk, doc_blk = inputs
        allowed = doc_blk[:, None] == row_doc[None, :]
        delta = jnp.sum(grad_blk.astype(jnp.float32) * output_blk.astype(jnp.float32), axis=3)
        query_parts = []
        key_parts = []
        value_parts = []
        for head in range(KVH):
            query_head = query_blk[:, head].astype(jnp.float32)
            grad_head = grad_blk[:, head].astype(jnp.float32)
            key_head = key_all[:, head]
            value_head = value_all[:, head]
            stat = jnp.transpose(stat_blk[:, head])[:, :, None]
            delta_head = jnp.transpose(delta[:, head])[:, :, None]
            score = jnp.einsum('tsd,id->sti', query_head, key_head) * scaling
            prob_full = jnp.where(allowed[None], jnp.exp(score - stat), 0.0)
            dprob = jnp.einsum('tsd,id->sti', grad_head, value_head)
            dscore = lax.optimization_barrier((prob_full * (dprob - delta_head) * scaling).astype(jnp.bfloat16)).astype(jnp.float32)
            prob_low = lax.optimization_barrier(prob_full.astype(jnp.bfloat16)).astype(jnp.float32)
            query_parts.append(jnp.einsum('sti,id->tsd', dscore, key_head))
            key_parts.append(jnp.einsum('sti,tsd->id', dscore, query_head))
            value_parts.append(jnp.einsum('sti,tsd->id', prob_low, grad_head))
        query_grad = jnp.stack(query_parts, axis=1).reshape(TOK_DEV, HEADS * DH).astype(jnp.bfloat16)
        dkey_sum = dkey_sum + jnp.stack(key_parts, axis=1)
        dvalue_sum = dvalue_sum + jnp.stack(value_parts, axis=1)
        return (dkey_sum, dvalue_sum), query_grad

    zeros_start = jnp.zeros((IMG_ROWS, KVH, DH), jnp.float32)
    (dkey_sum, dvalue_sum), query_grad = lax.scan(block_step, (zeros_start, zeros_start), (query_blocks, grad_blocks, output_blocks, stat_blocks, doc_blocks))
    kv_grad = jnp.stack([dkey_sum, dvalue_sum], axis=2).reshape(IMG_ROWS, KVH * 2 * DH).astype(jnp.bfloat16)
    return query_grad.reshape(TOKENS, HEADS * DH), kv_grad
```

```python
import functools
import math

import jax
import jax.numpy as jnp
from jax import lax
from jax.experimental import pallas as pl
from jax.experimental.pallas import tpu as pltpu
from jax.sharding import Mesh
from jax.sharding import PartitionSpec as P

BLK = ("z", "yl")
PATCH = ("x", "yh", "c")
DOC_SLOTS = 8
PAD_DOC = 7
GROUP = 4
MASKED = 1e30


def dot_nt(a, b):
    return lax.dot_general(a, b, (((1,), (1,)), ((), ())), preferred_element_type=jnp.float32)


def dot_nn(a, b):
    return lax.dot_general(a, b, (((1,), (0,)), ((), ())), preferred_element_type=jnp.float32)


def grad_kernel(span, block_docs, q_own, q_oth, g_own, g_oth, stat_own, stat_oth, docs, keys, values,
                dq_own, dq_oth, dkv, lse_doc, dq_acc, k_grp, v_grp, kt_grp, dk_acc, dv_acc, active, active_doc,
                *, heads, head_size):
    blocks, half_rows, _ = keys.shape
    scaling = head_size ** (-0.5)
    log2e = math.log2(math.e)

    doc_row = docs[...]
    for d in range(DOC_SLOTS):
        inside = doc_row == d
        for s, stat in enumerate((stat_own, stat_oth)):
            lse_doc[d, s * heads:(s + 1) * heads, :] = jnp.where(inside, stat[heads:, :] * log2e, MASKED)
    dq_acc[...] = jnp.zeros_like(dq_acc)
    dkv[...] = jnp.zeros_like(dkv)

    lowest, highest = span[0], span[1]

    def collect(b, count):
        doc = block_docs[b]
        active[count] = b
        active_doc[count] = doc
        return count + jnp.where((doc >= lowest) & (doc <= highest), 1, 0)

    count = lax.fori_loop(0, blocks, collect, jnp.int32(0))
    for s in range(GROUP):
        active[count + s] = 0
        active_doc[count + s] = PAD_DOC

    def group_step(grp, carry):
        base = grp * GROUP
        for s in range(GROUP):
            b = active[base + s]
            k_grp[s * half_rows:(s + 1) * half_rows, :] = keys[b]
            v_grp[s * half_rows:(s + 1) * half_rows, :] = values[b]
        kt_grp[...] = k_grp[...].T
        dk_acc[...] = jnp.zeros_like(dk_acc)
        dv_acc[...] = jnp.zeros_like(dv_acc)
        for h in range(2 * heads):
            q_ref, g_ref, stat = (q_own, g_own, stat_own) if h < heads else (q_oth, g_oth, stat_oth)
            col = (h % heads) * head_size
            query = q_ref[:, col:col + head_size]
            grad = g_ref[:, col:col + head_size]
            delta = stat[h % heads:h % heads + 1, :]
            score = dot_nt(k_grp[...], query)
            dprob = dot_nt(v_grp[...], grad)
            probs, dscores = [], []
            for s in range(GROUP):
                rows = slice(s * half_rows, (s + 1) * half_rows)
                stats = lse_doc[active_doc[base + s], h:h + 1, :]
                prob = jnp.exp2(score[rows] * (scaling * log2e) - stats)
                probs.append(prob.astype(jnp.bfloat16))
                dscores.append((prob * (dprob[rows] - delta) * scaling).astype(jnp.bfloat16))
            prob_low = jnp.concatenate(probs, axis=0)
            dscore = jnp.concatenate(dscores, axis=0)
            dk_acc[...] += dot_nn(dscore, query)
            dv_acc[...] += dot_nn(prob_low, grad)
            dq_acc[h] += dot_nn(kt_grp[...], dscore)
        for s in range(GROUP):
            rows = slice(s * half_rows, (s + 1) * half_rows)

            @pl.when(base + s < count)
            def _():
                b = active[base + s]
                dkv[b, :, :head_size] = dk_acc[rows, :].astype(jnp.bfloat16)
                dkv[b, :, head_size:] = dv_acc[rows, :].astype(jnp.bfloat16)

        return carry

    lax.fori_loop(0, (count + GROUP - 1) // GROUP, group_step, 0)
    for h in range(heads):
        dq_own[h] = dq_acc[h]
        dq_oth[h] = dq_acc[heads + h].astype(jnp.bfloat16)


def local_grads(span, block_docs, q_own, q_oth, g_own, g_oth, stat_own, stat_oth, docs, keys, values, interpret=False):
    tok, width = q_own.shape
    blocks, half_rows, head_size = keys.shape
    heads = width // head_size
    smem = pl.BlockSpec(memory_space=pltpu.SMEM)
    vmem = pl.BlockSpec(memory_space=pltpu.VMEM)
    rows = GROUP * half_rows
    return pl.pallas_call(
        functools.partial(grad_kernel, heads=heads, head_size=head_size),
        in_specs=[smem, smem] + [vmem] * 9,
        out_specs=[vmem] * 3,
        out_shape=[
            jax.ShapeDtypeStruct((heads, head_size, tok), jnp.float32),
            jax.ShapeDtypeStruct((heads, head_size, tok), jnp.bfloat16),
            jax.ShapeDtypeStruct((blocks, half_rows, 2 * head_size), jnp.bfloat16),
        ],
        scratch_shapes=[
            pltpu.VMEM((DOC_SLOTS, 2 * heads, tok), jnp.float32),
            pltpu.VMEM((2 * heads, head_size, tok), jnp.float32),
            pltpu.VMEM((rows, head_size), jnp.bfloat16),
            pltpu.VMEM((rows, head_size), jnp.bfloat16),
            pltpu.VMEM((head_size, rows), jnp.bfloat16),
            pltpu.VMEM((rows, head_size), jnp.float32),
            pltpu.VMEM((rows, head_size), jnp.float32),
            pltpu.SMEM((blocks + GROUP,), jnp.int32),
            pltpu.SMEM((blocks + GROUP,), jnp.int32),
        ],
        compiler_params=pltpu.CompilerParams(vmem_limit_bytes=40 << 20),
        interpret=interpret,
    )(span, block_docs, q_own, q_oth, g_own, g_oth, stat_own, stat_oth, docs, keys, values)


def body(queries, keys, values, outputs, out_grad, lse, doc_ids, image_docs):
    cores = lax.axis_size("c")
    owners = lax.axis_size("x") * lax.axis_size("yh")
    core = lax.axis_index("c")
    group_of = lax.axis_index(("x", "yh"))
    tok = queries.shape[0]
    heads = lse.shape[1]
    head_size = queries.shape[1] // heads
    block_rows = keys.shape[0]
    piece = block_rows // (owners * cores)
    half_rows = block_rows // cores
    swap = [(i, cores - 1 - i) for i in range(cores)]

    def mine(a):
        four = a.reshape(owners, cores, piece, a.shape[1])
        return lax.dynamic_slice(
            four, (0, core, 0, group_of * head_size), (owners, 1, piece, head_size)
        ).reshape(half_rows, head_size)

    both = jnp.concatenate([mine(keys), mine(values)], axis=1)
    plane = lax.all_gather(both, "yl", axis=0, tiled=True)
    key_all = lax.all_gather(plane[:, :head_size], "z", axis=0, tiled=True)
    value_all = lax.all_gather(plane[:, head_size:], "z", axis=0, tiled=True)

    delta = jnp.sum(
        out_grad.reshape(tok, heads, head_size).astype(jnp.float32)
        * outputs.reshape(tok, heads, head_size).astype(jnp.float32),
        axis=2,
    )
    stat_own = jnp.concatenate([delta, lse], axis=1).T
    q_oth = lax.ppermute(queries, "c", swap)
    g_oth = lax.ppermute(out_grad, "c", swap)
    stat_oth = lax.ppermute(stat_own, "c", swap)

    span = jnp.stack([doc_ids[0], doc_ids[tok - 1]])
    dq_own, dq_oth, dkv = local_grads(
        span, image_docs, queries, q_oth, out_grad, g_oth, stat_own, stat_oth, doc_ids[None, :],
        key_all.reshape(-1, half_rows, head_size), value_all.reshape(-1, half_rows, head_size),
    )
    dq_back = lax.ppermute(dq_oth, "c", swap)
    parts = lax.all_to_all(dkv, BLK, 0, 0, tiled=True)
    home = jnp.sum(parts.astype(jnp.float32), axis=0).astype(jnp.bfloat16)
    shares = lax.all_to_all(home.reshape(owners, piece, 2 * head_size), ("x", "yh"), 0, 0, tiled=True)
    kv_grad = jnp.transpose(shares, (1, 0, 2)).reshape(piece, owners * 2 * head_size)
    dquery = (dq_own + dq_back.astype(jnp.float32)).astype(jnp.bfloat16)
    query_grad = jnp.transpose(dquery, (2, 0, 1)).reshape(tok, heads * head_size)
    return (query_grad, kv_grad)


def solution(mesh):
    torus = Mesh(mesh.devices.reshape(12, 4, 4, 2, 2), BLK + PATCH)
    placed = (
        P(BLK, PATCH),
        P(BLK, None),
        P(BLK, None),
        P(BLK, PATCH),
        P(BLK, PATCH),
        P(BLK, PATCH),
        P(BLK),
        P(),
    )
    return jax.shard_map(
        body,
        mesh=torus,
        in_specs=placed,
        out_specs=(P(BLK, PATCH), P(BLK + PATCH, None)),
        check_vma=False,
    )
```

```python
import functools
import math

import jax
import jax.numpy as jnp
from jax import lax
from jax.experimental import pallas as pl
from jax.experimental.pallas import tpu as pltpu
from jax.sharding import Mesh
from jax.sharding import PartitionSpec as P

BLK = ("z", "yl")
PATCH = ("x", "yh", "c")
DOC_SLOTS = 8
PAD_DOC = 7
GROUP = 4
CHUNK = 256
MASKED = 1e30
SLOTS = 28
INFO_ROWS = 16
PIECES = 2


def dot_nt(a, b):
    return lax.dot_general(a, b, (((1,), (1,)), ((), ())), preferred_element_type=jnp.float32)


def dot_nn(a, b):
    return lax.dot_general(a, b, (((1,), (0,)), ((), ())), preferred_element_type=jnp.float32)


def ready_kernel(doc_ids, block_docs, where, keys, values, outputs, grads, lse, both, stats, table, order, tally,
                 *, owners, cores, cols, heads, head_size):
    blocks = block_docs.shape[0]
    block_rows = keys.shape[0]
    tok = grads.shape[0]
    half_rows = block_rows // cores
    piece = half_rows // (owners * cols)
    core, group = where[0], where[1]

    for d in range(DOC_SLOTS + 1):
        tally[d] = 0

    def count_one(b, carry):
        slot = block_docs[b] + 1
        tally[slot] = tally[slot] + 1
        return carry

    lax.fori_loop(0, blocks, count_one, 0)
    for d in range(1, DOC_SLOTS + 1):
        tally[d] = tally[d] + tally[d - 1]
    first = tally[doc_ids[0]]
    count = tally[doc_ids[tok - 1] + 1] - first

    def place(b, carry):
        doc = block_docs[b]
        at = tally[doc]
        tally[doc] = at + 1
        table[b] = at
        order[at] = b
        return carry

    lax.fori_loop(0, blocks, place, 0)
    order[blocks] = first
    order[blocks + 1] = count

    at = lax.broadcasted_iota(jnp.int32, (half_rows, block_rows), 0)
    row = lax.broadcasted_iota(jnp.int32, (half_rows, block_rows), 1)
    col, owner, sub = at // (owners * piece), at // piece % owners, at % piece
    pick = (row == ((owner * cores + core) * cols + col) * piece + sub).astype(jnp.float32).astype(jnp.bfloat16)
    lanes = pl.ds(pl.multiple_of(group * head_size, head_size), head_size)
    both[:half_rows, :head_size] = dot_nn(pick, keys[:, lanes]).astype(jnp.bfloat16)
    both[:half_rows, head_size:] = dot_nn(pick, values[:, lanes]).astype(jnp.bfloat16)
    lane = lax.broadcasted_iota(jnp.int32, (INFO_ROWS, 2 * head_size), 1)
    info = jnp.where(lane == 0, first, jnp.where(lane == 1, count, 0))
    both[half_rows:, :] = info.astype(jnp.float32).astype(jnp.bfloat16)

    lane = lax.broadcasted_iota(jnp.int32, (tok, head_size), 1)
    wide = jnp.zeros((tok, head_size), jnp.float32)
    for h in range(heads):
        span = slice(h * head_size, (h + 1) * head_size)
        product = grads[:, span].astype(jnp.float32) * outputs[:, span].astype(jnp.float32)
        wide = jnp.where(lane == h, jnp.sum(product, axis=1, keepdims=True), wide)
    stats[:heads, :] = wide.T[:heads, :]
    stats[heads:, :] = lse[...]


def ready(doc_ids, block_docs, where, keys, values, outputs, grads, lse, owners, cores, cols, interpret=False):
    heads, tok = lse.shape
    head_size = grads.shape[1] // heads
    blocks = block_docs.shape[0]
    half_rows = keys.shape[0] // cores
    smem = pl.BlockSpec(memory_space=pltpu.SMEM)
    vmem = pl.BlockSpec(memory_space=pltpu.VMEM)
    return pl.pallas_call(
        functools.partial(
            ready_kernel, owners=owners, cores=cores, cols=cols, heads=heads, head_size=head_size
        ),
        in_specs=[smem] * 3 + [vmem] * 5,
        out_specs=[vmem] * 2 + [smem] * 2,
        out_shape=[
            jax.ShapeDtypeStruct((half_rows + INFO_ROWS, 2 * head_size), jnp.bfloat16),
            jax.ShapeDtypeStruct((2 * heads, tok), jnp.float32),
            jax.ShapeDtypeStruct((blocks,), jnp.int32),
            jax.ShapeDtypeStruct((blocks + 2,), jnp.int32),
        ],
        scratch_shapes=[pltpu.SMEM((DOC_SLOTS + 1,), jnp.int32)],
        compiler_params=pltpu.CompilerParams(vmem_limit_bytes=12 << 20),
        interpret=interpret,
    )(doc_ids, block_docs, where, keys, values, outputs, grads, lse)


def grad_kernel(doc_ids, block_docs, order, plane, q_own, q_oth, g_own, g_oth, stat_own, stat_oth, docs, *refs,
                heads, head_size, half_rows, pieces):
    gathered, refs = refs[:pieces], refs[pieces:]
    dq_own, dq_oth, pack, rest, near, lse_doc, dq_acc, k_grp, v_grp, kt_grp, dk_acc, dv_acc = refs
    blocks = block_docs.shape[0]
    tile = half_rows + INFO_ROWS
    cols, piece_rows, _ = gathered[0].shape
    piece_planes = piece_rows // tile
    tok = docs.shape[1]
    part = half_rows // cols
    scaling = head_size ** (-0.5)
    log2e = math.log2(math.e)
    first, count = order[blocks], order[blocks + 1]

    lane = lax.broadcasted_iota(jnp.int32, (INFO_ROWS, head_size), 1)
    most = jnp.zeros((INFO_ROWS, head_size), jnp.float32)
    for col in range(cols):
        mate = jnp.zeros((INFO_ROWS, head_size), jnp.float32)
        for p, ref in enumerate(gathered):
            for z in range(piece_planes):
                info = ref[col, z * tile + half_rows:(z + 1) * tile, :head_size].astype(jnp.float32)
                most = jnp.maximum(most, info)
                mate = jnp.where(plane[0] == p * piece_planes + z, info, mate)
        near[col] = jnp.max(jnp.where(lane == 0, mate, 0.0)).astype(jnp.int32)
        near[cols + col] = jnp.max(jnp.where(lane == 1, mate, 0.0)).astype(jnp.int32)
    near[2 * cols] = jnp.max(jnp.where(lane == 1, most, 0.0)).astype(jnp.int32)

    doc_row = docs[...]
    for d in range(DOC_SLOTS):
        inside = doc_row == d
        for s, stat in enumerate((stat_own, stat_oth)):
            lse_doc[d, s * heads:(s + 1) * heads, :] = jnp.where(inside, stat[heads:, :] * log2e, MASKED)
    dq_acc[...] = jnp.zeros_like(dq_acc)
    pack[...] = jnp.zeros_like(pack)
    rest[...] = jnp.zeros_like(rest)

    def group_step(grp, carry):
        base = grp * GROUP
        group_docs = []
        for s in range(GROUP):
            b = order[first + jnp.minimum(base + s, count - 1)]
            col, at = lax.rem(b, cols), lax.div(b, cols)
            block = gathered[0][col, pl.ds(pl.multiple_of(jnp.minimum(at, piece_planes - 1) * tile, 16), half_rows), :]
            for p in range(1, pieces):
                near_at = jnp.clip(at - p * piece_planes, 0, piece_planes - 1)
                other = gathered[p][col, pl.ds(pl.multiple_of(near_at * tile, 16), half_rows), :]
                block = jnp.where(at >= p * piece_planes, other, block)
            k_grp[s * half_rows:(s + 1) * half_rows, :] = block[:, :head_size]
            v_grp[s * half_rows:(s + 1) * half_rows, :] = block[:, head_size:]
            group_docs.append(block_docs[b])
        slot_docs = [jnp.where(base + s < count, group_docs[s], PAD_DOC) for s in range(GROUP)]
        kt_grp[...] = k_grp[...].T
        dk_acc[...] = jnp.zeros_like(dk_acc)
        dv_acc[...] = jnp.zeros_like(dv_acc)
        for start in range(0, tok, CHUNK):
            toks = slice(start, start + CHUNK)

            @pl.when((group_docs[0] <= doc_ids[start + CHUNK - 1]) & (group_docs[-1] >= doc_ids[start]))
            def _():
                for h in range(2 * heads):
                    q_ref, g_ref, stat = (q_own, g_own, stat_own) if h < heads else (q_oth, g_oth, stat_oth)
                    at = (h % heads) * head_size
                    query = q_ref[toks, at:at + head_size]
                    grad = g_ref[toks, at:at + head_size]
                    delta = stat[h % heads:h % heads + 1, toks]
                    score = dot_nt(k_grp[...], query)
                    dprob = dot_nt(v_grp[...], grad)
                    probs, dscores = [], []
                    for s in range(GROUP):
                        rows = slice(s * half_rows, (s + 1) * half_rows)
                        stats = lse_doc[slot_docs[s], h:h + 1, toks]
                        prob = jnp.exp2(score[rows] * (scaling * log2e) - stats)
                        probs.append(prob.astype(jnp.bfloat16))
                        dscores.append((prob * (dprob[rows] - delta) * scaling).astype(jnp.bfloat16))
                    prob_low = jnp.concatenate(probs, axis=0)
                    dscore = jnp.concatenate(dscores, axis=0)
                    dk_acc[...] += dot_nn(dscore, query)
                    dv_acc[...] += dot_nn(prob_low, grad)
                    dq_acc[h, :, toks] += dot_nn(kt_grp[...], dscore)

        def put(out, slot):
            for s in range(GROUP):
                for j in range(cols):
                    rows = slice(s * half_rows + j * part, s * half_rows + (j + 1) * part)
                    out[j, slot + s, :, :head_size] = dk_acc[rows, :].astype(jnp.bfloat16)
                    out[j, slot + s, :, head_size:] = dv_acc[rows, :].astype(jnp.bfloat16)

        @pl.when(base < SLOTS)
        def _():
            put(pack, jnp.minimum(base, SLOTS - GROUP))

        @pl.when(base >= SLOTS)
        def _():
            put(rest, jnp.maximum(base - SLOTS, 0))

        return carry

    lax.fori_loop(0, (count + GROUP - 1) // GROUP, group_step, 0)
    for h in range(heads):
        dq_own[h] = dq_acc[h]
        dq_oth[h] = dq_acc[heads + h].astype(jnp.bfloat16)


def local_grads(doc_ids, block_docs, order, plane, q_own, q_oth, g_own, g_oth, stat_own, stat_oth, gathered, half_rows,
                interpret=False):
    tok, width = q_own.shape
    cols = gathered[0].shape[0]
    head_size = gathered[0].shape[2] // 2
    blocks = block_docs.shape[0]
    heads = width // head_size
    smem = pl.BlockSpec(memory_space=pltpu.SMEM)
    vmem = pl.BlockSpec(memory_space=pltpu.VMEM)
    rows = GROUP * half_rows
    return pl.pallas_call(
        functools.partial(grad_kernel, heads=heads, head_size=head_size, half_rows=half_rows, pieces=len(gathered)),
        in_specs=[smem] * 4 + [vmem] * (7 + len(gathered)),
        out_specs=[vmem] * 4 + [smem],
        out_shape=[
            jax.ShapeDtypeStruct((heads, head_size, tok), jnp.float32),
            jax.ShapeDtypeStruct((heads, head_size, tok), jnp.bfloat16),
            jax.ShapeDtypeStruct((cols, SLOTS, half_rows // cols, 2 * head_size), jnp.bfloat16),
            jax.ShapeDtypeStruct((cols, blocks - SLOTS, half_rows // cols, 2 * head_size), jnp.bfloat16),
            jax.ShapeDtypeStruct((2 * cols + 1,), jnp.int32),
        ],
        scratch_shapes=[
            pltpu.VMEM((DOC_SLOTS, 2 * heads, tok), jnp.float32),
            pltpu.VMEM((2 * heads, head_size, tok), jnp.float32),
            pltpu.VMEM((rows, head_size), jnp.bfloat16),
            pltpu.VMEM((rows, head_size), jnp.bfloat16),
            pltpu.VMEM((head_size, rows), jnp.bfloat16),
            pltpu.VMEM((rows, head_size), jnp.float32),
            pltpu.VMEM((rows, head_size), jnp.float32),
        ],
        compiler_params=pltpu.CompilerParams(vmem_limit_bytes=24 << 20),
        interpret=interpret,
    )(doc_ids, block_docs, order, plane, q_own, q_oth, g_own, g_oth, stat_own, stat_oth, doc_ids[None, :], *gathered)


def spread_kernel(table, near, *refs, blocks):
    pieces, out = refs[:-1], refs[-1]
    cols = pieces[0].shape[0]

    def step(b, carry):
        total = jnp.zeros(out.shape[1:], jnp.float32)
        for i in range(cols):
            slot = table[b] - near[i]
            begin = 0
            for piece in pieces:
                size = piece.shape[1]
                here = (slot >= begin) & (slot < jnp.minimum(near[cols + i], begin + size))
                part = piece[i, jnp.clip(slot - begin, 0, size - 1)].astype(jnp.float32)
                total = total + jnp.where(here, part, 0.0)
                begin += size
        out[b] = total.astype(jnp.bfloat16)
        return carry

    lax.fori_loop(0, blocks, step, 0, unroll=4)


def spread(table, near, pieces, blocks, interpret=False):
    smem = pl.BlockSpec(memory_space=pltpu.SMEM)
    vmem = pl.BlockSpec(memory_space=pltpu.VMEM)
    return pl.pallas_call(
        functools.partial(spread_kernel, blocks=blocks),
        in_specs=[smem] * 2 + [vmem] * len(pieces),
        out_specs=vmem,
        out_shape=jax.ShapeDtypeStruct((blocks,) + pieces[0].shape[2:], jnp.bfloat16),
        compiler_params=pltpu.CompilerParams(vmem_limit_bytes=12 << 20),
        interpret=interpret,
    )(table, near, *pieces)


def body(queries, keys, values, outputs, out_grad, lse, doc_ids, image_docs):
    cores = lax.axis_size("c")
    cols = lax.axis_size("yl")
    planes = lax.axis_size("z")
    owners = lax.axis_size("x") * lax.axis_size("yh")
    tok = queries.shape[0]
    heads = lse.shape[1]
    head_size = queries.shape[1] // heads
    blocks = image_docs.shape[0]
    half_rows = keys.shape[0] // cores
    piece = half_rows // (owners * cols)
    swap = [(i, cores - 1 - i) for i in range(cores)]

    where = jnp.stack([lax.axis_index("c"), lax.axis_index(("x", "yh"))]).astype(jnp.int32)
    both, stat_own, table, order = ready(
        doc_ids, image_docs, where, keys, values, outputs, out_grad, lse.T, owners, cores, cols
    )
    q_oth = lax.ppermute(queries, "c", swap)
    g_oth = lax.ppermute(out_grad, "c", swap)
    stat_oth = lax.ppermute(stat_own, "c", swap)

    column = lax.all_gather(both, "z", axis=0, tiled=True)
    cut = column.shape[0] // PIECES
    gathered = [lax.all_gather(column[p * cut:(p + 1) * cut], "yl", axis=0) for p in range(PIECES)]

    plane = lax.axis_index("z").astype(jnp.int32).reshape(1)
    dq_own, dq_oth, pack, rest, near = local_grads(
        doc_ids, image_docs, order, plane, queries, q_oth, out_grad, g_oth, stat_own, stat_oth, gathered, half_rows
    )
    dq_back = lax.ppermute(dq_oth, "c", swap)

    shared = lax.all_to_all(pack, "yl", 0, 0, tiled=True)

    def some(pieces):
        return spread(table, near, pieces[:1], blocks)

    def every(pieces):
        late = lax.all_to_all(pieces[1], "yl", 0, 0, tiled=True)
        return spread(table, near, (pieces[0], late), blocks)

    sums = lax.cond(near[2 * cols] <= SLOTS, some, every, (shared, rest))
    parts = lax.all_to_all(sums.reshape(planes, half_rows, 2 * head_size), "z", 0, 0, tiled=True)
    home = jnp.sum(parts.astype(jnp.float32), axis=0).astype(jnp.bfloat16)
    shares = lax.all_to_all(home.reshape(cols * owners, piece, 2 * head_size), ("yl", "x", "yh"), 0, 0, tiled=True)
    kv_grad = jnp.transpose(shares.reshape(cols, owners, piece, 2 * head_size), (0, 2, 1, 3)).reshape(
        cols * piece, owners * 2 * head_size
    )
    dquery = (dq_own + dq_back.astype(jnp.float32)).astype(jnp.bfloat16)
    query_grad = jnp.transpose(dquery, (2, 0, 1)).reshape(tok, heads * head_size)
    return (query_grad, kv_grad)


def solution(mesh):
    torus = Mesh(mesh.devices.reshape(12, 4, 4, 2, 2), BLK + PATCH)
    placed = (
        P(BLK, PATCH),
        P(BLK, None),
        P(BLK, None),
        P(BLK, PATCH),
        P(BLK, PATCH),
        P(BLK, PATCH),
        P(BLK),
        P(),
    )
    return jax.shard_map(
        body,
        mesh=torus,
        in_specs=placed,
        out_specs=(P(BLK, PATCH), P(BLK + PATCH, None)),
        check_vma=False,
    )
```

```python
import functools
import math

import jax
import jax.numpy as jnp
from jax import lax
from jax.experimental import pallas as pl
from jax.experimental.pallas import tpu as pltpu
from jax.sharding import Mesh
from jax.sharding import PartitionSpec as P

BLK = ("z", "yl")
PATCH = ("x", "yh", "c")
DOC_SLOTS = 8
PAD_DOC = 7
GROUP = 4
CHUNK = 256
MASKED = 1e30
SLOTS = 28
INFO_ROWS = 16
PIECES = 2
TERMS = 3
TERM_ROWS = 32


def dot_nt(a, b):
    return lax.dot_general(a, b, (((1,), (1,)), ((), ())), preferred_element_type=jnp.float32)


def dot_nn(a, b):
    return lax.dot_general(a, b, (((1,), (0,)), ((), ())), preferred_element_type=jnp.float32)


def in_hbm(*arrays):
    return [pltpu.with_memory_space_constraint(a, pltpu.HBM) for a in arrays]


def ready_kernel(doc_ids, block_docs, where, keys, values, queries, outputs, grads, lse, both, stats, swap, table, order,
                 tally, key_buf, value_buf, out_buf, grad_buf, terms, sems, *, owners, cores, cols, heads, head_size):
    blocks = block_docs.shape[0]
    block_rows = keys.shape[0]
    tok = grads.shape[0]
    half_rows = block_rows // cores
    piece = half_rows // (owners * cols)
    core, group = where[0], where[1]
    lanes = pl.ds(pl.multiple_of(group * head_size, head_size), head_size)
    copies = [
        pltpu.make_async_copy(grads, grad_buf, sems.at[0]),
        pltpu.make_async_copy(outputs, out_buf, sems.at[1]),
        pltpu.make_async_copy(keys.at[:, lanes], key_buf, sems.at[2]),
        pltpu.make_async_copy(values.at[:, lanes], value_buf, sems.at[3]),
        pltpu.make_async_copy(queries, swap.at[:tok, :], sems.at[4]),
        pltpu.make_async_copy(grads, swap.at[tok:2 * tok, :], sems.at[5]),
    ]
    for copy in copies:
        copy.start()

    for d in range(DOC_SLOTS + 1):
        tally[d] = 0

    def count_one(b, carry):
        slot = block_docs[b] + 1
        tally[slot] = tally[slot] + 1
        return carry

    lax.fori_loop(0, blocks, count_one, 0)
    for d in range(1, DOC_SLOTS + 1):
        tally[d] = tally[d] + tally[d - 1]
    first = tally[doc_ids[0]]
    count = tally[doc_ids[tok - 1] + 1] - first

    def place(b, carry):
        doc = block_docs[b]
        at = tally[doc]
        tally[doc] = at + 1
        table[b] = at
        order[at] = b
        return carry

    lax.fori_loop(0, blocks, place, 0)
    order[blocks] = first
    order[blocks + 1] = count

    copies[0].wait()
    copies[1].wait()
    lane = lax.broadcasted_iota(jnp.int32, (tok, head_size), 1)
    wide = jnp.zeros((tok, head_size), jnp.float32)
    for h in range(heads):
        span = slice(h * head_size, (h + 1) * head_size)
        product = grad_buf[:, span].astype(jnp.float32) * out_buf[:, span].astype(jnp.float32)
        wide = jnp.where(lane == h, jnp.sum(product, axis=1, keepdims=True), wide)
    full = jnp.concatenate([wide.T[:heads, :], lse[...]], axis=0)
    stats[...] = full
    terms[...] = jnp.zeros_like(terms)
    for t in range(TERMS):
        term = full.astype(jnp.bfloat16)
        terms[t * 2 * heads:(t + 1) * 2 * heads, :] = term
        full = full - term.astype(jnp.float32)
    last = pltpu.make_async_copy(terms, swap.at[2 * tok:, :], sems.at[6])
    last.start()

    at = lax.broadcasted_iota(jnp.int32, (half_rows, block_rows), 0)
    row = lax.broadcasted_iota(jnp.int32, (half_rows, block_rows), 1)
    col, owner, sub = at // (owners * piece), at // piece % owners, at % piece
    pick = (row == ((owner * cores + core) * cols + col) * piece + sub).astype(jnp.float32).astype(jnp.bfloat16)
    copies[2].wait()
    copies[3].wait()
    both[:half_rows, :head_size] = dot_nn(pick, key_buf[...]).astype(jnp.bfloat16)
    both[:half_rows, head_size:] = dot_nn(pick, value_buf[...]).astype(jnp.bfloat16)
    lane = lax.broadcasted_iota(jnp.int32, (INFO_ROWS, 2 * head_size), 1)
    info = jnp.where(lane == 0, first, jnp.where(lane == 1, count, 0))
    both[half_rows:, :] = info.astype(jnp.float32).astype(jnp.bfloat16)
    copies[4].wait()
    copies[5].wait()
    last.wait()


def ready(doc_ids, block_docs, where, keys, values, queries, outputs, grads, lse, owners, cores, cols, interpret=False):
    heads, tok = lse.shape
    width = grads.shape[1]
    head_size = width // heads
    blocks = block_docs.shape[0]
    block_rows = keys.shape[0]
    half_rows = block_rows // cores
    smem = pl.BlockSpec(memory_space=pltpu.SMEM)
    vmem = pl.BlockSpec(memory_space=pltpu.VMEM)
    hbm = pl.BlockSpec(memory_space=pltpu.HBM)
    return pl.pallas_call(
        functools.partial(
            ready_kernel, owners=owners, cores=cores, cols=cols, heads=heads, head_size=head_size
        ),
        in_specs=[smem] * 3 + [hbm] * 5 + [vmem],
        out_specs=[vmem] * 2 + [hbm] + [smem] * 2,
        out_shape=[
            jax.ShapeDtypeStruct((half_rows + INFO_ROWS, 2 * head_size), jnp.bfloat16),
            jax.ShapeDtypeStruct((2 * heads, tok), jnp.float32),
            pltpu.HBM((2 * tok + TERM_ROWS, width), jnp.bfloat16),
            jax.ShapeDtypeStruct((blocks,), jnp.int32),
            jax.ShapeDtypeStruct((blocks + 2,), jnp.int32),
        ],
        scratch_shapes=[
            pltpu.SMEM((DOC_SLOTS + 1,), jnp.int32),
            pltpu.VMEM((block_rows, head_size), jnp.bfloat16),
            pltpu.VMEM((block_rows, head_size), jnp.bfloat16),
            pltpu.VMEM((tok, width), jnp.bfloat16),
            pltpu.VMEM((tok, width), jnp.bfloat16),
            pltpu.VMEM((TERM_ROWS, width), jnp.bfloat16),
            pltpu.SemaphoreType.DMA((7,)),
        ],
        compiler_params=pltpu.CompilerParams(vmem_limit_bytes=12 << 20),
        interpret=interpret,
    )(doc_ids, block_docs, where, *in_hbm(keys, values, queries, outputs, grads), lse)


def grad_kernel(doc_ids, block_docs, order, plane, queries, grads, swapped, stat_own, docs, *refs,
                heads, head_size, half_rows, pieces):
    gathered, refs = refs[:pieces], refs[pieces:]
    dq_own, dq_out, pack_out, rest_out, near = refs[:5]
    lse_doc, dq_acc, dq_oth, pack, rest, q_all, g_all, terms, stats, k_grp, v_grp, kt_grp, dk_acc, dv_acc, sems = refs[5:]
    blocks = block_docs.shape[0]
    tile = half_rows + INFO_ROWS
    cols, piece_rows, _ = gathered[0].shape
    piece_planes = piece_rows // tile
    tok = docs.shape[1]
    part = half_rows // cols
    scaling = head_size ** (-0.5)
    log2e = math.log2(math.e)
    first, count = order[blocks], order[blocks + 1]
    loads = [pltpu.make_async_copy(swapped.at[2 * tok:, :], terms, sems.at[0])]
    for h in range(heads):
        span = slice(h * head_size, (h + 1) * head_size)
        loads += [
            pltpu.make_async_copy(queries.at[:, span], q_all.at[h], sems.at[1 + h]),
            pltpu.make_async_copy(grads.at[:, span], g_all.at[h], sems.at[1 + heads + h]),
            pltpu.make_async_copy(swapped.at[:tok, span], q_all.at[heads + h], sems.at[1 + 2 * heads + h]),
            pltpu.make_async_copy(swapped.at[tok:2 * tok, span], g_all.at[heads + h], sems.at[1 + 3 * heads + h]),
        ]
    for load in loads:
        load.start()

    lane = lax.broadcasted_iota(jnp.int32, (INFO_ROWS, head_size), 1)
    most = jnp.zeros((INFO_ROWS, head_size), jnp.float32)
    for col in range(cols):
        mate = jnp.zeros((INFO_ROWS, head_size), jnp.float32)
        for p, ref in enumerate(gathered):
            for z in range(piece_planes):
                info = ref[col, z * tile + half_rows:(z + 1) * tile, :head_size].astype(jnp.float32)
                most = jnp.maximum(most, info)
                mate = jnp.where(plane[0] == p * piece_planes + z, info, mate)
        near[col] = jnp.max(jnp.where(lane == 0, mate, 0.0)).astype(jnp.int32)
        near[cols + col] = jnp.max(jnp.where(lane == 1, mate, 0.0)).astype(jnp.int32)
    near[2 * cols] = jnp.max(jnp.where(lane == 1, most, 0.0)).astype(jnp.int32)

    loads[0].wait()
    theirs = jnp.zeros((2 * heads, tok), jnp.float32)
    for t in range(TERMS - 1, -1, -1):
        theirs = theirs + terms[t * 2 * heads:(t + 1) * 2 * heads, :].astype(jnp.float32)
    stats[:heads, :] = stat_own[:heads, :]
    stats[heads:, :] = theirs[:heads]
    lse_all = jnp.concatenate([stat_own[heads:, :], theirs[heads:]], axis=0) * log2e
    doc_row = docs[...]
    for d in range(DOC_SLOTS):
        lse_doc[d] = jnp.where(doc_row == d, lse_all, MASKED)
    dq_acc[...] = jnp.zeros_like(dq_acc)
    pack[...] = jnp.zeros_like(pack)

    @pl.when(count > SLOTS)
    def _():
        rest[...] = jnp.zeros_like(rest)

    for load in loads[1:]:
        load.wait()

    def group_step(grp, carry):
        base = grp * GROUP
        group_docs = []
        for s in range(GROUP):
            b = order[first + jnp.minimum(base + s, count - 1)]
            col, at = lax.rem(b, cols), lax.div(b, cols)
            block = gathered[0][col, pl.ds(pl.multiple_of(jnp.minimum(at, piece_planes - 1) * tile, 16), half_rows), :]
            for p in range(1, pieces):
                near_at = jnp.clip(at - p * piece_planes, 0, piece_planes - 1)
                other = gathered[p][col, pl.ds(pl.multiple_of(near_at * tile, 16), half_rows), :]
                block = jnp.where(at >= p * piece_planes, other, block)
            k_grp[s * half_rows:(s + 1) * half_rows, :] = block[:, :head_size]
            v_grp[s * half_rows:(s + 1) * half_rows, :] = block[:, head_size:]
            group_docs.append(block_docs[b])
        slot_docs = [jnp.where(base + s < count, group_docs[s], PAD_DOC) for s in range(GROUP)]
        kt_grp[...] = k_grp[...].T
        dk_acc[...] = jnp.zeros_like(dk_acc)
        dv_acc[...] = jnp.zeros_like(dv_acc)
        wanted = [
            (group_docs[0] <= doc_ids[start + CHUNK - 1]) & (group_docs[-1] >= doc_ids[start])
            for start in range(0, tok, CHUNK)
        ]

        def work(toks):
            for h in range(2 * heads):
                query = q_all[h, toks, :]
                grad = g_all[h, toks, :]
                delta = stats[h:h + 1, toks]
                score = dot_nt(k_grp[...], query)
                dprob = dot_nt(v_grp[...], grad)
                prob_low, dscore = [], []
                for s in range(GROUP):
                    rows = slice(s * half_rows, (s + 1) * half_rows)
                    shift = lse_doc[slot_docs[s], h:h + 1, toks]
                    prob = jnp.exp2(score[rows] * (scaling * log2e) - shift)
                    prob_low.append(prob.astype(jnp.bfloat16))
                    dscore.append((prob * (dprob[rows] - delta) * scaling).astype(jnp.bfloat16))
                low, ds = jnp.concatenate(prob_low, axis=0), jnp.concatenate(dscore, axis=0)
                dk_acc[...] += dot_nn(ds, query)
                dv_acc[...] += dot_nn(low, grad)
                dq_acc[h, :, toks] += dot_nn(kt_grp[...], ds)

        @pl.when(wanted[0] & wanted[1])
        def _():
            work(slice(0, tok))

        for i, other in ((0, 1), (1, 0)):

            @pl.when(wanted[i] & jnp.logical_not(wanted[other]))
            def _():
                work(slice(i * CHUNK, (i + 1) * CHUNK))

        def put(out, slot):
            for s in range(GROUP):
                for j in range(cols):
                    rows = slice(s * half_rows + j * part, s * half_rows + (j + 1) * part)
                    out[j, slot + s, :, :head_size] = dk_acc[rows, :].astype(jnp.bfloat16)
                    out[j, slot + s, :, head_size:] = dv_acc[rows, :].astype(jnp.bfloat16)

        @pl.when(base < SLOTS)
        def _():
            put(pack, jnp.minimum(base, SLOTS - GROUP))

        @pl.when(base >= SLOTS)
        def _():
            put(rest, jnp.maximum(base - SLOTS, 0))

        return carry

    lax.fori_loop(0, (count + GROUP - 1) // GROUP, group_step, 0)
    for h in range(heads):
        dq_own[h] = dq_acc[h]
        dq_oth[h] = dq_acc[heads + h].astype(jnp.bfloat16)
    stores = [
        pltpu.make_async_copy(pack, pack_out, sems.at[0]),
        pltpu.make_async_copy(dq_oth, dq_out, sems.at[1]),
    ]
    for store in stores:
        store.start()
    late = pltpu.make_async_copy(rest, rest_out, sems.at[2])

    @pl.when(count > SLOTS)
    def _():
        late.start()
        late.wait()

    for store in stores:
        store.wait()


def local_grads(doc_ids, block_docs, order, plane, queries, grads, swapped, stat_own, gathered, half_rows,
                interpret=False):
    tok, width = queries.shape
    cols = gathered[0].shape[0]
    head_size = gathered[0].shape[2] // 2
    blocks = block_docs.shape[0]
    heads = width // head_size
    smem = pl.BlockSpec(memory_space=pltpu.SMEM)
    vmem = pl.BlockSpec(memory_space=pltpu.VMEM)
    hbm = pl.BlockSpec(memory_space=pltpu.HBM)
    rows = GROUP * half_rows
    turned = (heads, head_size, tok)
    pack = (cols, SLOTS, half_rows // cols, 2 * head_size)
    rest = (cols, blocks - SLOTS, half_rows // cols, 2 * head_size)
    return pl.pallas_call(
        functools.partial(grad_kernel, heads=heads, head_size=head_size, half_rows=half_rows, pieces=len(gathered)),
        in_specs=[smem] * 4 + [hbm] * 2 + [pl.BlockSpec(memory_space=pl.ANY)] + [vmem] * (2 + len(gathered)),
        out_specs=[vmem] + [hbm] * 3 + [smem],
        out_shape=[
            jax.ShapeDtypeStruct(turned, jnp.float32),
            pltpu.HBM(turned, jnp.bfloat16),
            pltpu.HBM(pack, jnp.bfloat16),
            pltpu.HBM(rest, jnp.bfloat16),
            jax.ShapeDtypeStruct((2 * cols + 1,), jnp.int32),
        ],
        scratch_shapes=[
            pltpu.VMEM((DOC_SLOTS, 2 * heads, tok), jnp.float32),
            pltpu.VMEM((2 * heads, head_size, tok), jnp.float32),
            pltpu.VMEM(turned, jnp.bfloat16),
            pltpu.VMEM(pack, jnp.bfloat16),
            pltpu.VMEM(rest, jnp.bfloat16),
            pltpu.VMEM((2 * heads, tok, head_size), jnp.bfloat16),
            pltpu.VMEM((2 * heads, tok, head_size), jnp.bfloat16),
            pltpu.VMEM((TERM_ROWS, tok), jnp.bfloat16),
            pltpu.VMEM((2 * heads, tok), jnp.float32),
            pltpu.VMEM((rows, head_size), jnp.bfloat16),
            pltpu.VMEM((rows, head_size), jnp.bfloat16),
            pltpu.VMEM((head_size, rows), jnp.bfloat16),
            pltpu.VMEM((rows, head_size), jnp.float32),
            pltpu.VMEM((rows, head_size), jnp.float32),
            pltpu.SemaphoreType.DMA((1 + 4 * heads,)),
        ],
        compiler_params=pltpu.CompilerParams(vmem_limit_bytes=32 << 20),
        interpret=interpret,
    )(doc_ids, block_docs, order, plane, *in_hbm(queries, grads), swapped, stat_own, doc_ids[None, :], *gathered)


def spread_kernel(table, near, *refs, blocks):
    pieces, out = refs[:-1], refs[-1]
    cols = pieces[0].shape[0]

    def step(b, carry):
        total = jnp.zeros(out.shape[1:], jnp.float32)
        for i in range(cols):
            slot = table[b] - near[i]
            begin = 0
            for piece in pieces:
                size = piece.shape[1]
                here = (slot >= begin) & (slot < jnp.minimum(near[cols + i], begin + size))
                part = piece[i, jnp.clip(slot - begin, 0, size - 1)].astype(jnp.float32)
                total = total + jnp.where(here, part, 0.0)
                begin += size
        out[b] = total.astype(jnp.bfloat16)
        return carry

    lax.fori_loop(0, blocks, step, 0, unroll=4)


def spread(table, near, pieces, blocks, interpret=False):
    smem = pl.BlockSpec(memory_space=pltpu.SMEM)
    vmem = pl.BlockSpec(memory_space=pltpu.VMEM)
    return pl.pallas_call(
        functools.partial(spread_kernel, blocks=blocks),
        in_specs=[smem] * 2 + [vmem] * len(pieces),
        out_specs=vmem,
        out_shape=jax.ShapeDtypeStruct((blocks,) + pieces[0].shape[2:], jnp.bfloat16),
        compiler_params=pltpu.CompilerParams(vmem_limit_bytes=12 << 20),
        interpret=interpret,
    )(table, near, *pieces)


def body(queries, keys, values, outputs, out_grad, lse, doc_ids, image_docs):
    cores = lax.axis_size("c")
    cols = lax.axis_size("yl")
    planes = lax.axis_size("z")
    owners = lax.axis_size("x") * lax.axis_size("yh")
    tok = queries.shape[0]
    heads = lse.shape[1]
    head_size = queries.shape[1] // heads
    blocks = image_docs.shape[0]
    half_rows = keys.shape[0] // cores
    piece = half_rows // (owners * cols)
    swap = [(i, cores - 1 - i) for i in range(cores)]

    where = jnp.stack([lax.axis_index("c"), lax.axis_index(("x", "yh"))]).astype(jnp.int32)
    both, stat_own, swap_out, table, order = ready(
        doc_ids, image_docs, where, keys, values, queries, outputs, out_grad, lse.T, owners, cores, cols
    )
    swapped = lax.ppermute(swap_out, "c", swap)

    column = lax.all_gather(both, "z", axis=0, tiled=True)
    cut = column.shape[0] // PIECES
    gathered = [lax.all_gather(column[p * cut:(p + 1) * cut], "yl", axis=0) for p in range(PIECES)]

    plane = lax.axis_index("z").astype(jnp.int32).reshape(1)
    dq_own, dq_oth, pack, rest, near = local_grads(
        doc_ids, image_docs, order, plane, queries, out_grad, swapped, stat_own, gathered, half_rows
    )
    dq_back = lax.ppermute(dq_oth, "c", swap)

    shared = lax.all_to_all(pack, "yl", 0, 0, tiled=True)

    def some(pieces):
        return spread(table, near, pieces[:1], blocks)

    def every(pieces):
        late = lax.all_to_all(pieces[1], "yl", 0, 0, tiled=True)
        return spread(table, near, (pieces[0], late), blocks)

    sums = lax.cond(near[2 * cols] <= SLOTS, some, every, (shared, rest))
    parts = lax.all_to_all(sums.reshape(planes, half_rows, 2 * head_size), "z", 0, 0, tiled=True)
    home = jnp.sum(parts.astype(jnp.float32), axis=0).astype(jnp.bfloat16)
    shares = lax.all_to_all(home.reshape(cols * owners, piece, 2 * head_size), ("yl", "x", "yh"), 0, 0, tiled=True)
    kv_grad = jnp.transpose(shares.reshape(cols, owners, piece, 2 * head_size), (0, 2, 1, 3)).reshape(
        cols * piece, owners * 2 * head_size
    )
    dquery = (dq_own + dq_back.astype(jnp.float32)).astype(jnp.bfloat16)
    query_grad = jnp.transpose(dquery, (2, 0, 1)).reshape(tok, heads * head_size)
    return (query_grad, kv_grad)


def solution(mesh):
    torus = Mesh(mesh.devices.reshape(12, 4, 4, 2, 2), BLK + PATCH)
    placed = (
        P(BLK, PATCH),
        P(BLK, None),
        P(BLK, None),
        P(BLK, PATCH),
        P(BLK, PATCH),
        P(BLK, PATCH),
        P(BLK),
        P(),
    )
    return jax.shard_map(
        body,
        mesh=torus,
        in_specs=placed,
        out_specs=(P(BLK, PATCH), P(BLK + PATCH, None)),
        check_vma=False,
    )
```

```python
import functools
import math

import jax
import jax.numpy as jnp
from jax import lax
from jax.experimental import pallas as pl
from jax.experimental.pallas import tpu as pltpu
from jax.sharding import Mesh
from jax.sharding import PartitionSpec as P

BLK = ("z", "yl")
PATCH = ("x", "yh", "c")
DOC_SLOTS = 8
PAD_DOC = 7
GROUP = 4
CHUNK = 256
MASKED = 1e30
SLOTS = 28
INFO_ROWS = 16
PIECES = 2
TERMS = 3
TERM_ROWS = 32


def dot_nt(a, b):
    return lax.dot_general(a, b, (((1,), (1,)), ((), ())), preferred_element_type=jnp.float32)


def dot_nn(a, b):
    return lax.dot_general(a, b, (((1,), (0,)), ((), ())), preferred_element_type=jnp.float32)


def in_hbm(*arrays):
    return [pltpu.with_memory_space_constraint(a, pltpu.HBM) for a in arrays]


def ready_kernel(doc_ids, block_docs, where, keys, values, queries, outputs, grads, lse, both, stats, swap, table, order,
                 tally, key_buf, value_buf, out_buf, sems, *, owners, cores, cols, heads, head_size):
    blocks = block_docs.shape[0]
    block_rows = keys.shape[0]
    tok = grads.shape[0]
    half_rows = block_rows // cores
    piece = half_rows // (owners * cols)
    core, group = where[0], where[1]
    lanes = pl.ds(pl.multiple_of(group * head_size, head_size), head_size)
    copies = [
        pltpu.make_async_copy(grads, swap.at[tok:2 * tok, :], sems.at[0]),
        pltpu.make_async_copy(outputs, out_buf, sems.at[1]),
        pltpu.make_async_copy(keys.at[:, lanes], key_buf, sems.at[2]),
        pltpu.make_async_copy(values.at[:, lanes], value_buf, sems.at[3]),
        pltpu.make_async_copy(queries, swap.at[:tok, :], sems.at[4]),
    ]
    for copy in copies:
        copy.start()

    for d in range(DOC_SLOTS + 1):
        tally[d] = 0

    def count_one(b, carry):
        slot = block_docs[b] + 1
        tally[slot] = tally[slot] + 1
        return carry

    lax.fori_loop(0, blocks, count_one, 0)
    for d in range(1, DOC_SLOTS + 1):
        tally[d] = tally[d] + tally[d - 1]
    first = tally[doc_ids[0]]
    count = tally[doc_ids[tok - 1] + 1] - first

    def place(b, carry):
        doc = block_docs[b]
        at = tally[doc]
        tally[doc] = at + 1
        table[b] = at
        order[at] = b
        return carry

    lax.fori_loop(0, blocks, place, 0)
    order[blocks] = first
    order[blocks + 1] = count

    copies[0].wait()
    copies[1].wait()
    lane = lax.broadcasted_iota(jnp.int32, (tok, head_size), 1)
    wide = jnp.zeros((tok, head_size), jnp.float32)
    for h in range(heads):
        span = slice(h * head_size, (h + 1) * head_size)
        product = swap[tok:2 * tok, span].astype(jnp.float32) * out_buf[:, span].astype(jnp.float32)
        wide = jnp.where(lane == h, jnp.sum(product, axis=1, keepdims=True), wide)
    full = jnp.concatenate([wide.T[:heads, :], lse[...]], axis=0)
    stats[...] = full
    swap[2 * tok:, :] = jnp.zeros((TERM_ROWS, tok), jnp.bfloat16)
    for t in range(TERMS):
        term = full.astype(jnp.bfloat16)
        swap[2 * tok + t * 2 * heads:2 * tok + (t + 1) * 2 * heads, :] = term
        full = full - term.astype(jnp.float32)

    at = lax.broadcasted_iota(jnp.int32, (half_rows, block_rows), 0)
    row = lax.broadcasted_iota(jnp.int32, (half_rows, block_rows), 1)
    col, owner, sub = at // (owners * piece), at // piece % owners, at % piece
    pick = (row == ((owner * cores + core) * cols + col) * piece + sub).astype(jnp.float32).astype(jnp.bfloat16)
    copies[2].wait()
    copies[3].wait()
    both[:half_rows, :head_size] = dot_nn(pick, key_buf[...]).astype(jnp.bfloat16)
    both[:half_rows, head_size:] = dot_nn(pick, value_buf[...]).astype(jnp.bfloat16)
    lane = lax.broadcasted_iota(jnp.int32, (INFO_ROWS, 2 * head_size), 1)
    info = jnp.where(lane == 0, first, jnp.where(lane == 1, count, 0))
    both[half_rows:, :] = info.astype(jnp.float32).astype(jnp.bfloat16)
    copies[4].wait()


def ready(doc_ids, block_docs, where, keys, values, queries, outputs, grads, lse, owners, cores, cols, interpret=False):
    heads, tok = lse.shape
    width = grads.shape[1]
    head_size = width // heads
    blocks = block_docs.shape[0]
    block_rows = keys.shape[0]
    half_rows = block_rows // cores
    smem = pl.BlockSpec(memory_space=pltpu.SMEM)
    vmem = pl.BlockSpec(memory_space=pltpu.VMEM)
    hbm = pl.BlockSpec(memory_space=pltpu.HBM)
    return pl.pallas_call(
        functools.partial(
            ready_kernel, owners=owners, cores=cores, cols=cols, heads=heads, head_size=head_size
        ),
        in_specs=[smem] * 3 + [hbm] * 5 + [vmem],
        out_specs=[vmem] * 3 + [smem] * 2,
        out_shape=[
            jax.ShapeDtypeStruct((half_rows + INFO_ROWS, 2 * head_size), jnp.bfloat16),
            jax.ShapeDtypeStruct((2 * heads, tok), jnp.float32),
            jax.ShapeDtypeStruct((2 * tok + TERM_ROWS, width), jnp.bfloat16),
            jax.ShapeDtypeStruct((blocks,), jnp.int32),
            jax.ShapeDtypeStruct((blocks + 2,), jnp.int32),
        ],
        scratch_shapes=[
            pltpu.SMEM((DOC_SLOTS + 1,), jnp.int32),
            pltpu.VMEM((block_rows, head_size), jnp.bfloat16),
            pltpu.VMEM((block_rows, head_size), jnp.bfloat16),
            pltpu.VMEM((tok, width), jnp.bfloat16),
            pltpu.SemaphoreType.DMA((5,)),
        ],
        compiler_params=pltpu.CompilerParams(vmem_limit_bytes=12 << 20),
        interpret=interpret,
    )(doc_ids, block_docs, where, *in_hbm(keys, values, queries, outputs, grads), lse)


def grad_kernel(doc_ids, block_docs, order, plane, queries, grads, swapped, stat_own, docs, *refs,
                heads, head_size, half_rows, pieces):
    gathered, refs = refs[:pieces], refs[pieces:]
    dq_own, dq_out, pack_out, rest_out, near = refs[:5]
    lse_doc, dq_acc, dq_oth, pack, rest, q_all, g_all, terms, stats, k_grp, v_grp, kt_grp, dk_acc, dv_acc, sems = refs[5:]
    blocks = block_docs.shape[0]
    tile = half_rows + INFO_ROWS
    cols, piece_rows, _ = gathered[0].shape
    piece_planes = piece_rows // tile
    tok = docs.shape[1]
    part = half_rows // cols
    scaling = head_size ** (-0.5)
    log2e = math.log2(math.e)
    first, count = order[blocks], order[blocks + 1]
    loads = [pltpu.make_async_copy(swapped.at[2 * tok:, :], terms, sems.at[0])]
    for h in range(heads):
        span = slice(h * head_size, (h + 1) * head_size)
        loads += [
            pltpu.make_async_copy(queries.at[:, span], q_all.at[h], sems.at[1 + h]),
            pltpu.make_async_copy(grads.at[:, span], g_all.at[h], sems.at[1 + heads + h]),
            pltpu.make_async_copy(swapped.at[:tok, span], q_all.at[heads + h], sems.at[1 + 2 * heads + h]),
            pltpu.make_async_copy(swapped.at[tok:2 * tok, span], g_all.at[heads + h], sems.at[1 + 3 * heads + h]),
        ]
    for load in loads:
        load.start()

    lane = lax.broadcasted_iota(jnp.int32, (INFO_ROWS, head_size), 1)
    most = jnp.zeros((INFO_ROWS, head_size), jnp.float32)
    for col in range(cols):
        mate = jnp.zeros((INFO_ROWS, head_size), jnp.float32)
        for p, ref in enumerate(gathered):
            for z in range(piece_planes):
                info = ref[col, z * tile + half_rows:(z + 1) * tile, :head_size].astype(jnp.float32)
                most = jnp.maximum(most, info)
                mate = jnp.where(plane[0] == p * piece_planes + z, info, mate)
        near[col] = jnp.max(jnp.where(lane == 0, mate, 0.0)).astype(jnp.int32)
        near[cols + col] = jnp.max(jnp.where(lane == 1, mate, 0.0)).astype(jnp.int32)
    near[2 * cols] = jnp.max(jnp.where(lane == 1, most, 0.0)).astype(jnp.int32)

    loads[0].wait()
    theirs = jnp.zeros((2 * heads, tok), jnp.float32)
    for t in range(TERMS - 1, -1, -1):
        theirs = theirs + terms[t * 2 * heads:(t + 1) * 2 * heads, :].astype(jnp.float32)
    stats[:heads, :] = stat_own[:heads, :]
    stats[heads:, :] = theirs[:heads]
    lse_all = jnp.concatenate([stat_own[heads:, :], theirs[heads:]], axis=0) * log2e
    doc_row = docs[...]
    for d in range(DOC_SLOTS):
        lse_doc[d] = jnp.where(doc_row == d, lse_all, MASKED)
    dq_acc[...] = jnp.zeros_like(dq_acc)
    pack[...] = jnp.zeros_like(pack)

    @pl.when(count > SLOTS)
    def _():
        rest[...] = jnp.zeros_like(rest)

    for load in loads[1:]:
        load.wait()

    def group_step(grp, carry):
        base = grp * GROUP
        group_docs = []
        for s in range(GROUP):
            b = order[first + jnp.minimum(base + s, count - 1)]
            col, at = lax.rem(b, cols), lax.div(b, cols)
            block = gathered[0][col, pl.ds(pl.multiple_of(jnp.minimum(at, piece_planes - 1) * tile, 16), half_rows), :]
            for p in range(1, pieces):
                near_at = jnp.clip(at - p * piece_planes, 0, piece_planes - 1)
                other = gathered[p][col, pl.ds(pl.multiple_of(near_at * tile, 16), half_rows), :]
                block = jnp.where(at >= p * piece_planes, other, block)
            k_grp[s * half_rows:(s + 1) * half_rows, :] = block[:, :head_size]
            v_grp[s * half_rows:(s + 1) * half_rows, :] = block[:, head_size:]
            group_docs.append(block_docs[b])
        slot_docs = [jnp.where(base + s < count, group_docs[s], PAD_DOC) for s in range(GROUP)]
        kt_grp[...] = k_grp[...].T
        dk_acc[...] = jnp.zeros_like(dk_acc)
        dv_acc[...] = jnp.zeros_like(dv_acc)
        wanted = [
            (group_docs[0] <= doc_ids[start + CHUNK - 1]) & (group_docs[-1] >= doc_ids[start])
            for start in range(0, tok, CHUNK)
        ]

        def work(toks):
            for h in range(2 * heads):
                query = q_all[h, toks, :]
                grad = g_all[h, toks, :]
                delta = stats[h:h + 1, toks]
                score = dot_nt(k_grp[...], query)
                dprob = dot_nt(v_grp[...], grad)
                prob_low, dscore = [], []
                for s in range(GROUP):
                    rows = slice(s * half_rows, (s + 1) * half_rows)
                    shift = lse_doc[slot_docs[s], h:h + 1, toks]
                    prob = jnp.exp2(score[rows] * (scaling * log2e) - shift)
                    prob_low.append(prob.astype(jnp.bfloat16))
                    dscore.append((prob * (dprob[rows] - delta) * scaling).astype(jnp.bfloat16))
                low, ds = jnp.concatenate(prob_low, axis=0), jnp.concatenate(dscore, axis=0)
                dk_acc[...] += dot_nn(ds, query)
                dv_acc[...] += dot_nn(low, grad)
                dq_acc[h, :, toks] += dot_nn(kt_grp[...], ds)

        @pl.when(wanted[0] & wanted[1])
        def _():
            work(slice(0, tok))

        for i, other in ((0, 1), (1, 0)):

            @pl.when(wanted[i] & jnp.logical_not(wanted[other]))
            def _():
                work(slice(i * CHUNK, (i + 1) * CHUNK))

        def put(out, slot):
            for s in range(GROUP):
                for j in range(cols):
                    rows = slice(s * half_rows + j * part, s * half_rows + (j + 1) * part)
                    out[j, slot + s, :, :head_size] = dk_acc[rows, :].astype(jnp.bfloat16)
                    out[j, slot + s, :, head_size:] = dv_acc[rows, :].astype(jnp.bfloat16)

        @pl.when(base < SLOTS)
        def _():
            put(pack, jnp.minimum(base, SLOTS - GROUP))

        @pl.when(base >= SLOTS)
        def _():
            put(rest, jnp.maximum(base - SLOTS, 0))

        return carry

    lax.fori_loop(0, (count + GROUP - 1) // GROUP, group_step, 0)
    for h in range(heads):
        dq_own[h] = dq_acc[h]
        dq_oth[h] = dq_acc[heads + h].astype(jnp.bfloat16)
    stores = [
        pltpu.make_async_copy(pack, pack_out, sems.at[0]),
        pltpu.make_async_copy(dq_oth, dq_out, sems.at[1]),
    ]
    for store in stores:
        store.start()
    late = pltpu.make_async_copy(rest, rest_out, sems.at[2])

    @pl.when(count > SLOTS)
    def _():
        late.start()
        late.wait()

    for store in stores:
        store.wait()


def local_grads(doc_ids, block_docs, order, plane, queries, grads, swapped, stat_own, gathered, half_rows,
                interpret=False):
    tok, width = queries.shape
    cols = gathered[0].shape[0]
    head_size = gathered[0].shape[2] // 2
    blocks = block_docs.shape[0]
    heads = width // head_size
    smem = pl.BlockSpec(memory_space=pltpu.SMEM)
    vmem = pl.BlockSpec(memory_space=pltpu.VMEM)
    hbm = pl.BlockSpec(memory_space=pltpu.HBM)
    rows = GROUP * half_rows
    turned = (heads, head_size, tok)
    pack = (cols, SLOTS, half_rows // cols, 2 * head_size)
    rest = (cols, blocks - SLOTS, half_rows // cols, 2 * head_size)
    return pl.pallas_call(
        functools.partial(grad_kernel, heads=heads, head_size=head_size, half_rows=half_rows, pieces=len(gathered)),
        in_specs=[smem] * 4 + [hbm] * 2 + [pl.BlockSpec(memory_space=pl.ANY)] + [vmem] * (2 + len(gathered)),
        out_specs=[vmem] + [hbm] * 3 + [smem],
        out_shape=[
            jax.ShapeDtypeStruct(turned, jnp.float32),
            pltpu.HBM(turned, jnp.bfloat16),
            pltpu.HBM(pack, jnp.bfloat16),
            pltpu.HBM(rest, jnp.bfloat16),
            jax.ShapeDtypeStruct((2 * cols + 1,), jnp.int32),
        ],
        scratch_shapes=[
            pltpu.VMEM((DOC_SLOTS, 2 * heads, tok), jnp.float32),
            pltpu.VMEM((2 * heads, head_size, tok), jnp.float32),
            pltpu.VMEM(turned, jnp.bfloat16),
            pltpu.VMEM(pack, jnp.bfloat16),
            pltpu.VMEM(rest, jnp.bfloat16),
            pltpu.VMEM((2 * heads, tok, head_size), jnp.bfloat16),
            pltpu.VMEM((2 * heads, tok, head_size), jnp.bfloat16),
            pltpu.VMEM((TERM_ROWS, tok), jnp.bfloat16),
            pltpu.VMEM((2 * heads, tok), jnp.float32),
            pltpu.VMEM((rows, head_size), jnp.bfloat16),
            pltpu.VMEM((rows, head_size), jnp.bfloat16),
            pltpu.VMEM((head_size, rows), jnp.bfloat16),
            pltpu.VMEM((rows, head_size), jnp.float32),
            pltpu.VMEM((rows, head_size), jnp.float32),
            pltpu.SemaphoreType.DMA((1 + 4 * heads,)),
        ],
        compiler_params=pltpu.CompilerParams(vmem_limit_bytes=32 << 20),
        interpret=interpret,
    )(doc_ids, block_docs, order, plane, *in_hbm(queries, grads), swapped, stat_own, doc_ids[None, :], *gathered)


def spread_kernel(table, near, *refs, blocks):
    pieces, out = refs[:-1], refs[-1]
    cols = pieces[0].shape[0]

    def step(b, carry):
        total = jnp.zeros(out.shape[1:], jnp.float32)
        for i in range(cols):
            slot = table[b] - near[i]
            begin = 0
            for piece in pieces:
                size = piece.shape[1]
                here = (slot >= begin) & (slot < jnp.minimum(near[cols + i], begin + size))
                part = piece[i, jnp.clip(slot - begin, 0, size - 1)].astype(jnp.float32)
                total = total + jnp.where(here, part, 0.0)
                begin += size
        out[b] = total.astype(jnp.bfloat16)
        return carry

    lax.fori_loop(0, blocks, step, 0, unroll=4)


def spread(table, near, pieces, blocks, interpret=False):
    smem = pl.BlockSpec(memory_space=pltpu.SMEM)
    vmem = pl.BlockSpec(memory_space=pltpu.VMEM)
    return pl.pallas_call(
        functools.partial(spread_kernel, blocks=blocks),
        in_specs=[smem] * 2 + [vmem] * len(pieces),
        out_specs=vmem,
        out_shape=jax.ShapeDtypeStruct((blocks,) + pieces[0].shape[2:], jnp.bfloat16),
        compiler_params=pltpu.CompilerParams(vmem_limit_bytes=12 << 20),
        interpret=interpret,
    )(table, near, *pieces)


def body(queries, keys, values, outputs, out_grad, lse, doc_ids, image_docs):
    cores = lax.axis_size("c")
    cols = lax.axis_size("yl")
    planes = lax.axis_size("z")
    owners = lax.axis_size("x") * lax.axis_size("yh")
    tok = queries.shape[0]
    heads = lse.shape[1]
    head_size = queries.shape[1] // heads
    blocks = image_docs.shape[0]
    half_rows = keys.shape[0] // cores
    piece = half_rows // (owners * cols)
    swap = [(i, cores - 1 - i) for i in range(cores)]

    where = jnp.stack([lax.axis_index("c"), lax.axis_index(("x", "yh"))]).astype(jnp.int32)
    both, stat_own, swap_out, table, order = ready(
        doc_ids, image_docs, where, keys, values, queries, outputs, out_grad, lse.T, owners, cores, cols
    )
    swapped = lax.ppermute(swap_out, "c", swap)

    column = lax.all_gather(both, "z", axis=0, tiled=True)
    cut = column.shape[0] // PIECES
    gathered = [lax.all_gather(column[p * cut:(p + 1) * cut], "yl", axis=0) for p in range(PIECES)]

    plane = lax.axis_index("z").astype(jnp.int32).reshape(1)
    dq_own, dq_oth, pack, rest, near = local_grads(
        doc_ids, image_docs, order, plane, queries, out_grad, swapped, stat_own, gathered, half_rows
    )
    dq_back = lax.ppermute(dq_oth, "c", swap)

    shared = lax.all_to_all(pack, "yl", 0, 0, tiled=True)

    def some(pieces):
        return spread(table, near, pieces[:1], blocks)

    def every(pieces):
        late = lax.all_to_all(pieces[1], "yl", 0, 0, tiled=True)
        return spread(table, near, (pieces[0], late), blocks)

    sums = lax.cond(near[2 * cols] <= SLOTS, some, every, (shared, rest))
    parts = lax.all_to_all(sums.reshape(planes, half_rows, 2 * head_size), "z", 0, 0, tiled=True)
    home = jnp.sum(parts.astype(jnp.float32), axis=0).astype(jnp.bfloat16)
    shares = lax.all_to_all(home.reshape(cols * owners, piece, 2 * head_size), ("yl", "x", "yh"), 0, 0, tiled=True)
    kv_grad = jnp.transpose(shares.reshape(cols, owners, piece, 2 * head_size), (0, 2, 1, 3)).reshape(
        cols * piece, owners * 2 * head_size
    )
    dquery = (dq_own + dq_back.astype(jnp.float32)).astype(jnp.bfloat16)
    query_grad = jnp.transpose(dquery, (2, 0, 1)).reshape(tok, heads * head_size)
    return (query_grad, kv_grad)


def solution(mesh):
    torus = Mesh(mesh.devices.reshape(12, 4, 4, 2, 2), BLK + PATCH)
    placed = (
        P(BLK, PATCH),
        P(BLK, None),
        P(BLK, None),
        P(BLK, PATCH),
        P(BLK, PATCH),
        P(BLK, PATCH),
        P(BLK),
        P(),
    )
    return jax.shard_map(
        body,
        mesh=torus,
        in_specs=placed,
        out_specs=(P(BLK, PATCH), P(BLK + PATCH, None)),
        check_vma=False,
    )
```

```python
import functools
import math

import jax
import jax.numpy as jnp
from jax import lax
from jax.experimental import pallas as pl
from jax.experimental.pallas import tpu as pltpu
from jax.sharding import Mesh
from jax.sharding import PartitionSpec as P

BLK = ("z", "yl")
PATCH = ("x", "yh", "c")
DOC_SLOTS = 8
PAD_DOC = 7
GROUP = 4
CHUNK = 256
MASKED = 1e30
SLOTS = 28
INFO_ROWS = 16
PIECE_PLANES = 6
TERMS = 3
TERM_ROWS = 32


def dot_nt(a, b):
    return lax.dot_general(a, b, (((1,), (1,)), ((), ())), preferred_element_type=jnp.float32)


def dot_nn(a, b):
    return lax.dot_general(a, b, (((1,), (0,)), ((), ())), preferred_element_type=jnp.float32)


def in_hbm(*arrays):
    return [pltpu.with_memory_space_constraint(a, pltpu.HBM) for a in arrays]


def ready_kernel(where, doc_hbm, block_hbm, keys, values, queries, outputs, grads, lse_hbm, both, stats, swap, table, order,
                 tally, doc_ids, block_docs, lse, key_buf, value_buf, out_buf, sems, *, owners, cores, cols, heads, head_size):
    blocks = block_docs.shape[0]
    block_rows = keys.shape[0]
    tok = grads.shape[0]
    half_rows = block_rows // cores
    piece = half_rows // (owners * cols)
    core, group = where[0], where[1]
    lanes = pl.ds(pl.multiple_of(group * head_size, head_size), head_size)
    copies = [
        pltpu.make_async_copy(grads, swap.at[tok:2 * tok, :], sems.at[0]),
        pltpu.make_async_copy(outputs, out_buf, sems.at[1]),
        pltpu.make_async_copy(keys.at[:, lanes], key_buf, sems.at[2]),
        pltpu.make_async_copy(values.at[:, lanes], value_buf, sems.at[3]),
        pltpu.make_async_copy(queries, swap.at[:tok, :], sems.at[4]),
        pltpu.make_async_copy(block_hbm, block_docs, sems.at[5]),
        pltpu.make_async_copy(doc_hbm, doc_ids, sems.at[6]),
        pltpu.make_async_copy(lse_hbm, lse, sems.at[7]),
    ]
    for copy in copies[5:] + copies[:5]:
        copy.start()
    copies[5].wait()
    copies[6].wait()

    for d in range(DOC_SLOTS + 1):
        tally[d] = 0

    def count_one(b, carry):
        slot = block_docs[b] + 1
        tally[slot] = tally[slot] + 1
        return carry

    lax.fori_loop(0, blocks, count_one, 0)
    for d in range(1, DOC_SLOTS + 1):
        tally[d] = tally[d] + tally[d - 1]
    first = tally[doc_ids[0]]
    count = tally[doc_ids[tok - 1] + 1] - first

    def place(b, carry):
        doc = block_docs[b]
        at = tally[doc]
        tally[doc] = at + 1
        table[b] = at
        order[at] = b
        return carry

    lax.fori_loop(0, blocks, place, 0)
    order[blocks] = first
    order[blocks + 1] = count

    copies[0].wait()
    copies[1].wait()
    copies[7].wait()
    lane = lax.broadcasted_iota(jnp.int32, (tok, head_size), 1)
    wide = jnp.zeros((tok, head_size), jnp.float32)
    for h in range(heads):
        span = slice(h * head_size, (h + 1) * head_size)
        product = swap[tok:2 * tok, span].astype(jnp.float32) * out_buf[:, span].astype(jnp.float32)
        wide = jnp.where(lane == h, jnp.sum(product, axis=1, keepdims=True), wide)
    full = jnp.concatenate([wide.T[:heads, :], lse[...]], axis=0)
    stats[...] = full
    swap[2 * tok:, :] = jnp.zeros((TERM_ROWS, tok), jnp.bfloat16)
    for t in range(TERMS):
        term = full.astype(jnp.bfloat16)
        swap[2 * tok + t * 2 * heads:2 * tok + (t + 1) * 2 * heads, :] = term
        full = full - term.astype(jnp.float32)

    at = lax.broadcasted_iota(jnp.int32, (half_rows, block_rows), 0)
    row = lax.broadcasted_iota(jnp.int32, (half_rows, block_rows), 1)
    col, owner, sub = at // (owners * piece), at // piece % owners, at % piece
    pick = (row == ((owner * cores + core) * cols + col) * piece + sub).astype(jnp.float32).astype(jnp.bfloat16)
    copies[2].wait()
    copies[3].wait()
    both[:half_rows, :head_size] = dot_nn(pick, key_buf[...]).astype(jnp.bfloat16)
    both[:half_rows, head_size:] = dot_nn(pick, value_buf[...]).astype(jnp.bfloat16)
    lane = lax.broadcasted_iota(jnp.int32, (INFO_ROWS, 2 * head_size), 1)
    info = jnp.where(lane == 0, first, jnp.where(lane == 1, count, 0))
    both[half_rows:, :] = info.astype(jnp.float32).astype(jnp.bfloat16)
    copies[4].wait()


def ready(doc_ids, block_docs, where, keys, values, queries, outputs, grads, lse, owners, cores, cols, interpret=False):
    heads, tok = lse.shape
    width = grads.shape[1]
    head_size = width // heads
    blocks = block_docs.shape[0]
    block_rows = keys.shape[0]
    half_rows = block_rows // cores
    smem = pl.BlockSpec(memory_space=pltpu.SMEM)
    vmem = pl.BlockSpec(memory_space=pltpu.VMEM)
    hbm = pl.BlockSpec(memory_space=pltpu.HBM)
    return pl.pallas_call(
        functools.partial(
            ready_kernel, owners=owners, cores=cores, cols=cols, heads=heads, head_size=head_size
        ),
        in_specs=[smem] + [hbm] * 8,
        out_specs=[vmem] * 3 + [smem] * 2,
        out_shape=[
            jax.ShapeDtypeStruct((half_rows + INFO_ROWS, 2 * head_size), jnp.bfloat16),
            jax.ShapeDtypeStruct((2 * heads, tok), jnp.float32),
            jax.ShapeDtypeStruct((2 * tok + TERM_ROWS, width), jnp.bfloat16),
            jax.ShapeDtypeStruct((blocks,), jnp.int32),
            jax.ShapeDtypeStruct((blocks + 2,), jnp.int32),
        ],
        scratch_shapes=[
            pltpu.SMEM((DOC_SLOTS + 1,), jnp.int32),
            pltpu.SMEM((tok,), jnp.int32),
            pltpu.SMEM((blocks,), jnp.int32),
            pltpu.VMEM((heads, tok), jnp.float32),
            pltpu.VMEM((block_rows, head_size), jnp.bfloat16),
            pltpu.VMEM((block_rows, head_size), jnp.bfloat16),
            pltpu.VMEM((tok, width), jnp.bfloat16),
            pltpu.SemaphoreType.DMA((8,)),
        ],
        compiler_params=pltpu.CompilerParams(vmem_limit_bytes=12 << 20),
        interpret=interpret,
    )(where, *in_hbm(doc_ids, block_docs, keys, values, queries, outputs, grads, lse))


def trim_kernel(column, *pieces):
    tile = column.shape[0] // (len(pieces) * PIECE_PLANES)
    half_rows = tile - INFO_ROWS
    row = lax.broadcasted_iota(jnp.int32, (INFO_ROWS, column.shape[1]), 0)
    info = jnp.zeros((INFO_ROWS, column.shape[1]), jnp.float32)
    for p, piece in enumerate(pieces):
        for k in range(PIECE_PLANES):
            z = p * PIECE_PLANES + k
            piece[k * half_rows:(k + 1) * half_rows, :] = column[z * tile:z * tile + half_rows, :]
            info = jnp.where(row == z, column[z * tile + half_rows:(z + 1) * tile, :].astype(jnp.float32), info)
    pieces[0][PIECE_PLANES * half_rows:, :] = info.astype(jnp.bfloat16)


def trim(column, half_rows, planes, interpret=False):
    vmem = pl.BlockSpec(memory_space=pltpu.VMEM)
    rows = PIECE_PLANES * half_rows
    sizes = [rows + INFO_ROWS] + [rows] * (planes // PIECE_PLANES - 1)
    return pl.pallas_call(
        trim_kernel,
        in_specs=[vmem],
        out_specs=[vmem] * len(sizes),
        out_shape=[jax.ShapeDtypeStruct((n, column.shape[1]), jnp.bfloat16) for n in sizes],
        compiler_params=pltpu.CompilerParams(vmem_limit_bytes=4 << 20),
        interpret=interpret,
    )(column)


def grad_kernel(doc_ids, block_docs, order, plane, queries, grads, swapped, stat_own, docs, *refs,
                heads, head_size, half_rows, pieces):
    gathered, refs = refs[:pieces], refs[pieces:]
    dq_own, dq_out, pack_out, rest_out, near = refs[:5]
    lse_doc, dq_acc, dq_oth, pack, rest, q_all, g_all, terms, stats, k_grp, v_grp, kt_grp, dk_acc, dv_acc, sems = refs[5:]
    blocks = block_docs.shape[0]
    cols = gathered[0].shape[0]
    tok = docs.shape[1]
    part = half_rows // cols
    scaling = head_size ** (-0.5)
    log2e = math.log2(math.e)
    first, count = order[blocks], order[blocks + 1]
    loads = [pltpu.make_async_copy(swapped.at[2 * tok:, :], terms, sems.at[0])]
    for h in range(heads):
        span = slice(h * head_size, (h + 1) * head_size)
        loads += [
            pltpu.make_async_copy(queries.at[:, span], q_all.at[h], sems.at[1 + h]),
            pltpu.make_async_copy(grads.at[:, span], g_all.at[h], sems.at[1 + heads + h]),
            pltpu.make_async_copy(swapped.at[:tok, span], q_all.at[heads + h], sems.at[1 + 2 * heads + h]),
            pltpu.make_async_copy(swapped.at[tok:2 * tok, span], g_all.at[heads + h], sems.at[1 + 3 * heads + h]),
        ]
    for load in loads:
        load.start()

    lane = lax.broadcasted_iota(jnp.int32, (INFO_ROWS, head_size), 1)
    row = lax.broadcasted_iota(jnp.int32, (INFO_ROWS, head_size), 0)
    most = jnp.zeros((INFO_ROWS, head_size), jnp.float32)
    for col in range(cols):
        info = gathered[0][col, PIECE_PLANES * half_rows:, :head_size].astype(jnp.float32)
        most = jnp.maximum(most, info)
        mine = row == plane[0]
        near[col] = jnp.max(jnp.where(mine & (lane == 0), info, 0.0)).astype(jnp.int32)
        near[cols + col] = jnp.max(jnp.where(mine & (lane == 1), info, 0.0)).astype(jnp.int32)
    near[2 * cols] = jnp.max(jnp.where(lane == 1, most, 0.0)).astype(jnp.int32)

    loads[0].wait()
    theirs = jnp.zeros((2 * heads, tok), jnp.float32)
    for t in range(TERMS - 1, -1, -1):
        theirs = theirs + terms[t * 2 * heads:(t + 1) * 2 * heads, :].astype(jnp.float32)
    stats[:heads, :] = stat_own[:heads, :]
    stats[heads:, :] = theirs[:heads]
    lse_all = jnp.concatenate([stat_own[heads:, :], theirs[heads:]], axis=0) * log2e
    doc_row = docs[...]
    for d in range(DOC_SLOTS):
        lse_doc[d] = jnp.where(doc_row == d, lse_all, MASKED)
    dq_own[...] = jnp.zeros_like(dq_own)
    dq_acc[...] = jnp.zeros_like(dq_acc)
    pack[...] = jnp.zeros_like(pack)

    @pl.when(count > SLOTS)
    def _():
        rest[...] = jnp.zeros_like(rest)

    for load in loads[1:]:
        load.wait()

    def group_step(grp, carry):
        base = grp * GROUP
        group_docs = []
        for s in range(GROUP):
            b = order[first + jnp.minimum(base + s, count - 1)]
            col, at = lax.rem(b, cols), lax.div(b, cols)
            block = None
            for p in range(pieces):
                row = jnp.clip(at - p * PIECE_PLANES, 0, PIECE_PLANES - 1) * half_rows
                found = gathered[p][col, pl.ds(pl.multiple_of(row, half_rows), half_rows), :]
                block = found if p == 0 else jnp.where(at >= p * PIECE_PLANES, found, block)
            k_grp[s * half_rows:(s + 1) * half_rows, :] = block[:, :head_size]
            v_grp[s * half_rows:(s + 1) * half_rows, :] = block[:, head_size:]
            group_docs.append(block_docs[b])
        slot_docs = [jnp.where(base + s < count, group_docs[s], PAD_DOC) for s in range(GROUP)]
        kt_grp[...] = k_grp[...].T
        dk_acc[...] = jnp.zeros_like(dk_acc)
        dv_acc[...] = jnp.zeros_like(dv_acc)
        wanted = [
            (group_docs[0] <= doc_ids[start + CHUNK - 1]) & (group_docs[-1] >= doc_ids[start])
            for start in range(0, tok, CHUNK)
        ]

        def work(toks):
            for h in range(2 * heads):
                query = q_all[h, toks, :]
                grad = g_all[h, toks, :]
                delta = stats[h:h + 1, toks]
                score = dot_nt(k_grp[...], query)
                dprob = dot_nt(v_grp[...], grad)
                prob_low, dscore = [], []
                for s in range(GROUP):
                    rows = slice(s * half_rows, (s + 1) * half_rows)
                    shift = lse_doc[slot_docs[s], h:h + 1, toks]
                    prob = jnp.exp2(score[rows] * (scaling * log2e) - shift)
                    prob_low.append(prob.astype(jnp.bfloat16))
                    dscore.append((prob * (dprob[rows] - delta) * scaling).astype(jnp.bfloat16))
                low, ds = jnp.concatenate(prob_low, axis=0), jnp.concatenate(dscore, axis=0)
                dk_acc[...] += dot_nn(ds, query)
                dv_acc[...] += dot_nn(low, grad)
                turned = dot_nn(kt_grp[...], ds)
                if h < heads:
                    dq_own[h, :, toks] += turned
                else:
                    dq_acc[h - heads, :, toks] += turned

        @pl.when(wanted[0] & wanted[1])
        def _():
            work(slice(0, tok))

        for i, other in ((0, 1), (1, 0)):

            @pl.when(wanted[i] & jnp.logical_not(wanted[other]))
            def _():
                work(slice(i * CHUNK, (i + 1) * CHUNK))

        def put(out, slot):
            for s in range(GROUP):
                for j in range(cols):
                    rows = slice(s * half_rows + j * part, s * half_rows + (j + 1) * part)
                    out[j, slot + s, :, :head_size] = dk_acc[rows, :].astype(jnp.bfloat16)
                    out[j, slot + s, :, head_size:] = dv_acc[rows, :].astype(jnp.bfloat16)

        @pl.when(base < SLOTS)
        def _():
            put(pack, jnp.minimum(base, SLOTS - GROUP))

        @pl.when(base >= SLOTS)
        def _():
            put(rest, jnp.maximum(base - SLOTS, 0))

        return carry

    lax.fori_loop(0, (count + GROUP - 1) // GROUP, group_step, 0)
    for h in range(heads):
        dq_oth[h] = dq_acc[h].astype(jnp.bfloat16)
    stores = [
        pltpu.make_async_copy(pack, pack_out, sems.at[0]),
        pltpu.make_async_copy(dq_oth, dq_out, sems.at[1]),
    ]
    for store in stores:
        store.start()
    late = pltpu.make_async_copy(rest, rest_out, sems.at[2])

    @pl.when(count > SLOTS)
    def _():
        late.start()
        late.wait()

    for store in stores:
        store.wait()


def local_grads(doc_ids, block_docs, order, plane, queries, grads, swapped, stat_own, gathered, half_rows,
                interpret=False):
    tok, width = queries.shape
    cols = gathered[0].shape[0]
    head_size = gathered[0].shape[2] // 2
    blocks = block_docs.shape[0]
    heads = width // head_size
    smem = pl.BlockSpec(memory_space=pltpu.SMEM)
    vmem = pl.BlockSpec(memory_space=pltpu.VMEM)
    hbm = pl.BlockSpec(memory_space=pltpu.HBM)
    rows = GROUP * half_rows
    turned = (heads, head_size, tok)
    pack = (cols, SLOTS, half_rows // cols, 2 * head_size)
    rest = (cols, blocks - SLOTS, half_rows // cols, 2 * head_size)
    return pl.pallas_call(
        functools.partial(grad_kernel, heads=heads, head_size=head_size, half_rows=half_rows, pieces=len(gathered)),
        in_specs=[smem] * 4 + [hbm] * 2 + [pl.BlockSpec(memory_space=pl.ANY)] + [vmem] * (2 + len(gathered)),
        out_specs=[vmem] + [hbm] * 3 + [smem],
        out_shape=[
            jax.ShapeDtypeStruct(turned, jnp.float32),
            pltpu.HBM(turned, jnp.bfloat16),
            pltpu.HBM(pack, jnp.bfloat16),
            pltpu.HBM(rest, jnp.bfloat16),
            jax.ShapeDtypeStruct((2 * cols + 1,), jnp.int32),
        ],
        scratch_shapes=[
            pltpu.VMEM((DOC_SLOTS, 2 * heads, tok), jnp.float32),
            pltpu.VMEM(turned, jnp.float32),
            pltpu.VMEM(turned, jnp.bfloat16),
            pltpu.VMEM(pack, jnp.bfloat16),
            pltpu.VMEM(rest, jnp.bfloat16),
            pltpu.VMEM((2 * heads, tok, head_size), jnp.bfloat16),
            pltpu.VMEM((2 * heads, tok, head_size), jnp.bfloat16),
            pltpu.VMEM((TERM_ROWS, tok), jnp.bfloat16),
            pltpu.VMEM((2 * heads, tok), jnp.float32),
            pltpu.VMEM((rows, head_size), jnp.bfloat16),
            pltpu.VMEM((rows, head_size), jnp.bfloat16),
            pltpu.VMEM((head_size, rows), jnp.bfloat16),
            pltpu.VMEM((rows, head_size), jnp.float32),
            pltpu.VMEM((rows, head_size), jnp.float32),
            pltpu.SemaphoreType.DMA((1 + 4 * heads,)),
        ],
        compiler_params=pltpu.CompilerParams(vmem_limit_bytes=32 << 20),
        interpret=interpret,
    )(doc_ids, block_docs, order, plane, *in_hbm(queries, grads), swapped, stat_own, doc_ids[None, :], *gathered)


def spread_kernel(table, near, *refs, blocks):
    pieces, out = refs[:-1], refs[-1]
    cols = pieces[0].shape[0]

    def step(b, carry):
        total = jnp.zeros(out.shape[1:], jnp.float32)
        for i in range(cols):
            slot = table[b] - near[i]
            begin = 0
            for piece in pieces:
                size = piece.shape[1]
                here = (slot >= begin) & (slot < jnp.minimum(near[cols + i], begin + size))
                part = piece[i, jnp.clip(slot - begin, 0, size - 1)].astype(jnp.float32)
                total = total + jnp.where(here, part, 0.0)
                begin += size
        out[b] = total.astype(jnp.bfloat16)
        return carry

    lax.fori_loop(0, blocks, step, 0, unroll=4)


def spread(table, near, pieces, blocks, interpret=False):
    smem = pl.BlockSpec(memory_space=pltpu.SMEM)
    vmem = pl.BlockSpec(memory_space=pltpu.VMEM)
    return pl.pallas_call(
        functools.partial(spread_kernel, blocks=blocks),
        in_specs=[smem] * 2 + [vmem] * len(pieces),
        out_specs=vmem,
        out_shape=jax.ShapeDtypeStruct((blocks,) + pieces[0].shape[2:], jnp.bfloat16),
        compiler_params=pltpu.CompilerParams(vmem_limit_bytes=12 << 20),
        interpret=interpret,
    )(table, near, *pieces)


def body(queries, keys, values, outputs, out_grad, lse, doc_ids, image_docs):
    cores = lax.axis_size("c")
    cols = lax.axis_size("yl")
    planes = lax.axis_size("z")
    owners = lax.axis_size("x") * lax.axis_size("yh")
    tok = queries.shape[0]
    heads = lse.shape[1]
    head_size = queries.shape[1] // heads
    blocks = image_docs.shape[0]
    half_rows = keys.shape[0] // cores
    piece = half_rows // (owners * cols)
    swap = [(i, cores - 1 - i) for i in range(cores)]

    where = jnp.stack([lax.axis_index("c"), lax.axis_index(("x", "yh"))]).astype(jnp.int32)
    both, stat_own, swap_out, table, order = ready(
        doc_ids, image_docs, where, keys, values, queries, outputs, out_grad, lse.T, owners, cores, cols
    )
    swapped = lax.ppermute(swap_out, "c", swap)

    column = lax.all_gather(both, "z", axis=0, tiled=True)
    gathered = [lax.all_gather(p, "yl", axis=0) for p in trim(column, half_rows, planes)]

    plane = lax.axis_index("z").astype(jnp.int32).reshape(1)
    dq_own, dq_oth, pack, rest, near = local_grads(
        doc_ids, image_docs, order, plane, queries, out_grad, swapped, stat_own, gathered, half_rows
    )
    dq_back = lax.ppermute(dq_oth, "c", swap)

    shared = lax.all_to_all(pack, "yl", 0, 0, tiled=True)

    def some(pieces):
        return spread(table, near, pieces[:1], blocks)

    def every(pieces):
        late = lax.all_to_all(pieces[1], "yl", 0, 0, tiled=True)
        return spread(table, near, (pieces[0], late), blocks)

    sums = lax.cond(near[2 * cols] <= SLOTS, some, every, (shared, rest))
    parts = lax.all_to_all(sums.reshape(planes, half_rows, 2 * head_size), "z", 0, 0, tiled=True)
    home = jnp.sum(parts.astype(jnp.float32), axis=0).astype(jnp.bfloat16)
    shares = lax.all_to_all(home.reshape(cols * owners, piece, 2 * head_size), ("yl", "x", "yh"), 0, 0, tiled=True)
    kv_grad = jnp.transpose(shares.reshape(cols, owners, piece, 2 * head_size), (0, 2, 1, 3)).reshape(
        cols * piece, owners * 2 * head_size
    )
    dquery = (dq_own + dq_back.astype(jnp.float32)).astype(jnp.bfloat16)
    query_grad = jnp.transpose(dquery, (2, 0, 1)).reshape(tok, heads * head_size)
    return (query_grad, kv_grad)


def solution(mesh):
    torus = Mesh(mesh.devices.reshape(12, 4, 4, 2, 2), BLK + PATCH)
    placed = (
        P(BLK, PATCH),
        P(BLK, None),
        P(BLK, None),
        P(BLK, PATCH),
        P(BLK, PATCH),
        P(BLK, PATCH),
        P(BLK),
        P(),
    )
    return jax.shard_map(
        body,
        mesh=torus,
        in_specs=placed,
        out_specs=(P(BLK, PATCH), P(BLK + PATCH, None)),
        check_vma=False,
    )
```

```python
import functools
import math

import jax
import jax.numpy as jnp
from jax import lax
from jax.experimental import pallas as pl
from jax.experimental.pallas import tpu as pltpu
from jax.sharding import Mesh
from jax.sharding import PartitionSpec as P

BLK = ("z", "yl")
PATCH = ("x", "yh", "c")
DOC_SLOTS = 8
PAD_DOC = 7
GROUP = 4
CHUNK = 256
MASKED = 1e30
SLOTS = 28
INFO_ROWS = 16
TERMS = 3
TERM_ROWS = 32


def dot_nt(a, b):
    return lax.dot_general(a, b, (((1,), (1,)), ((), ())), preferred_element_type=jnp.float32)


def dot_nn(a, b):
    return lax.dot_general(a, b, (((1,), (0,)), ((), ())), preferred_element_type=jnp.float32)


def in_hbm(*arrays):
    return [pltpu.with_memory_space_constraint(a, pltpu.HBM) for a in arrays]


def ready_kernel(where, doc_hbm, block_hbm, keys, values, queries, outputs, grads, lse_hbm, both, stats, swap, table, order,
                 tally, doc_ids, block_docs, lse, key_buf, value_buf, out_buf, sems, *, owners, cores, cols, heads, head_size):
    blocks = block_docs.shape[0]
    block_rows = keys.shape[0]
    tok = grads.shape[0]
    half_rows = block_rows // cores
    piece = half_rows // (owners * cols)
    core, group = where[0], where[1]
    lanes = pl.ds(pl.multiple_of(group * head_size, head_size), head_size)
    copies = [
        pltpu.make_async_copy(grads, swap.at[tok:2 * tok, :], sems.at[0]),
        pltpu.make_async_copy(outputs, out_buf, sems.at[1]),
        pltpu.make_async_copy(keys.at[:, lanes], key_buf, sems.at[2]),
        pltpu.make_async_copy(values.at[:, lanes], value_buf, sems.at[3]),
        pltpu.make_async_copy(queries, swap.at[:tok, :], sems.at[4]),
        pltpu.make_async_copy(block_hbm, block_docs, sems.at[5]),
        pltpu.make_async_copy(doc_hbm, doc_ids, sems.at[6]),
        pltpu.make_async_copy(lse_hbm, lse, sems.at[7]),
    ]
    for copy in copies[5:] + copies[:5]:
        copy.start()
    copies[5].wait()
    copies[6].wait()

    for d in range(DOC_SLOTS + 1):
        tally[d] = 0

    def count_one(b, carry):
        slot = block_docs[b] + 1
        tally[slot] = tally[slot] + 1
        return carry

    lax.fori_loop(0, blocks, count_one, 0)
    for d in range(1, DOC_SLOTS + 1):
        tally[d] = tally[d] + tally[d - 1]
    first = tally[doc_ids[0]]
    count = tally[doc_ids[tok - 1] + 1] - first

    def place(b, carry):
        doc = block_docs[b]
        at = tally[doc]
        tally[doc] = at + 1
        table[b] = at
        order[at] = b
        return carry

    lax.fori_loop(0, blocks, place, 0)
    order[blocks] = first
    order[blocks + 1] = count

    copies[0].wait()
    copies[1].wait()
    copies[7].wait()
    lane = lax.broadcasted_iota(jnp.int32, (tok, head_size), 1)
    wide = jnp.zeros((tok, head_size), jnp.float32)
    for h in range(heads):
        span = slice(h * head_size, (h + 1) * head_size)
        product = swap[tok:2 * tok, span].astype(jnp.float32) * out_buf[:, span].astype(jnp.float32)
        wide = jnp.where(lane == h, jnp.sum(product, axis=1, keepdims=True), wide)
    full = jnp.concatenate([wide.T[:heads, :], lse[...]], axis=0)
    stats[...] = full
    swap[2 * tok:, :] = jnp.zeros((TERM_ROWS, tok), jnp.bfloat16)
    for t in range(TERMS):
        term = full.astype(jnp.bfloat16)
        swap[2 * tok + t * 2 * heads:2 * tok + (t + 1) * 2 * heads, :] = term
        full = full - term.astype(jnp.float32)

    at = lax.broadcasted_iota(jnp.int32, (half_rows, block_rows), 0)
    row = lax.broadcasted_iota(jnp.int32, (half_rows, block_rows), 1)
    col, owner, sub = at // (owners * piece), at // piece % owners, at % piece
    pick = (row == ((owner * cores + core) * cols + col) * piece + sub).astype(jnp.float32).astype(jnp.bfloat16)
    copies[2].wait()
    copies[3].wait()
    part = half_rows // cols
    key_rows = dot_nn(pick, key_buf[...]).astype(jnp.bfloat16)
    value_rows = dot_nn(pick, value_buf[...]).astype(jnp.bfloat16)
    lane = lax.broadcasted_iota(jnp.int32, (INFO_ROWS, 2 * head_size), 1)
    info = jnp.where(lane == 0, first, jnp.where(lane == 1, count, 0))
    for j in range(cols):
        both[j, :part, :head_size] = key_rows[j * part:(j + 1) * part]
        both[j, :part, head_size:] = value_rows[j * part:(j + 1) * part]
        both[j, part:, :] = info.astype(jnp.float32).astype(jnp.bfloat16)
    copies[4].wait()


def ready(doc_ids, block_docs, where, keys, values, queries, outputs, grads, lse, owners, cores, cols, interpret=False):
    heads, tok = lse.shape
    width = grads.shape[1]
    head_size = width // heads
    blocks = block_docs.shape[0]
    block_rows = keys.shape[0]
    half_rows = block_rows // cores
    smem = pl.BlockSpec(memory_space=pltpu.SMEM)
    vmem = pl.BlockSpec(memory_space=pltpu.VMEM)
    hbm = pl.BlockSpec(memory_space=pltpu.HBM)
    return pl.pallas_call(
        functools.partial(
            ready_kernel, owners=owners, cores=cores, cols=cols, heads=heads, head_size=head_size
        ),
        in_specs=[smem] + [hbm] * 8,
        out_specs=[vmem] * 3 + [smem] * 2,
        out_shape=[
            jax.ShapeDtypeStruct((cols, half_rows // cols + INFO_ROWS, 2 * head_size), jnp.bfloat16),
            jax.ShapeDtypeStruct((2 * heads, tok), jnp.float32),
            jax.ShapeDtypeStruct((2 * tok + TERM_ROWS, width), jnp.bfloat16),
            jax.ShapeDtypeStruct((blocks,), jnp.int32),
            jax.ShapeDtypeStruct((blocks + 2,), jnp.int32),
        ],
        scratch_shapes=[
            pltpu.SMEM((DOC_SLOTS + 1,), jnp.int32),
            pltpu.SMEM((tok,), jnp.int32),
            pltpu.SMEM((blocks,), jnp.int32),
            pltpu.VMEM((heads, tok), jnp.float32),
            pltpu.VMEM((block_rows, head_size), jnp.bfloat16),
            pltpu.VMEM((block_rows, head_size), jnp.bfloat16),
            pltpu.VMEM((tok, width), jnp.bfloat16),
            pltpu.SemaphoreType.DMA((8,)),
        ],
        compiler_params=pltpu.CompilerParams(vmem_limit_bytes=12 << 20),
        interpret=interpret,
    )(where, *in_hbm(doc_ids, block_docs, keys, values, queries, outputs, grads, lse))


def join_kernel(chunks, joined):
    cols = chunks.shape[0]
    part = chunks.shape[1] - INFO_ROWS
    row = lax.broadcasted_iota(jnp.int32, (INFO_ROWS, chunks.shape[2]), 0)
    info = jnp.zeros((INFO_ROWS, chunks.shape[2]), jnp.float32)
    for i in range(cols):
        joined[i * part:(i + 1) * part, :] = chunks[i, :part, :]
        info = jnp.where(row == i, chunks[i, part:, :].astype(jnp.float32), info)
    joined[cols * part:, :] = info.astype(jnp.bfloat16)


def join(chunks, interpret=False):
    vmem = pl.BlockSpec(memory_space=pltpu.VMEM)
    cols, rows, width = chunks.shape
    return pl.pallas_call(
        join_kernel,
        in_specs=[vmem],
        out_specs=vmem,
        out_shape=jax.ShapeDtypeStruct((cols * (rows - INFO_ROWS) + INFO_ROWS, width), jnp.bfloat16),
        compiler_params=pltpu.CompilerParams(vmem_limit_bytes=4 << 20),
        interpret=interpret,
    )(chunks)


def choose_kernel(order, plane, column, wanted, late, near, *, planes, blocks):
    cols, slots, part, width = wanted.shape
    tile = cols * part + INFO_ROWS
    lane = lax.broadcasted_iota(jnp.int32, (INFO_ROWS, width), 1)
    row = lax.broadcasted_iota(jnp.int32, (INFO_ROWS, width), 0)
    most = jnp.zeros((INFO_ROWS, width), jnp.float32)
    for z in range(planes):
        most = jnp.maximum(most, column[z * tile + cols * part:(z + 1) * tile, :].astype(jnp.float32))
    most = jnp.max(jnp.where(lane == 1, most, 0.0)).astype(jnp.int32)
    near[2 * cols] = most
    info = column[pl.ds(pl.multiple_of(plane[0] * tile + cols * part, 16), INFO_ROWS), :].astype(jnp.float32)
    for i in range(cols):
        near[i] = jnp.max(jnp.where((row == i) & (lane == 0), info, 0.0)).astype(jnp.int32)
        near[cols + i] = jnp.max(jnp.where((row == i) & (lane == 1), info, 0.0)).astype(jnp.int32)

    def fill(out, begin):
        def step(k, carry):
            for i in range(cols):
                b = order[jnp.minimum(near[i] + begin + k, blocks - 1)]
                at = pl.multiple_of(lax.div(b, cols) * tile + lax.rem(b, cols) * part, 16)
                out[i, k] = column[pl.ds(at, part), :]
            return carry

        lax.fori_loop(0, out.shape[1], step, 0, unroll=2)

    fill(wanted, 0)

    @pl.when(most > slots)
    def _():
        fill(late, slots)


def choose(order, plane, column, planes, cols, blocks, interpret=False):
    smem = pl.BlockSpec(memory_space=pltpu.SMEM)
    vmem = pl.BlockSpec(memory_space=pltpu.VMEM)
    part = (column.shape[0] // planes - INFO_ROWS) // cols
    return pl.pallas_call(
        functools.partial(choose_kernel, planes=planes, blocks=blocks),
        in_specs=[smem] * 2 + [vmem],
        out_specs=[vmem] * 2 + [smem],
        out_shape=[
            jax.ShapeDtypeStruct((cols, SLOTS, part, column.shape[1]), jnp.bfloat16),
            jax.ShapeDtypeStruct((cols, blocks - SLOTS, part, column.shape[1]), jnp.bfloat16),
            jax.ShapeDtypeStruct((2 * cols + 1,), jnp.int32),
        ],
        compiler_params=pltpu.CompilerParams(vmem_limit_bytes=8 << 20),
        interpret=interpret,
    )(order, plane, column)


def grad_kernel(doc_ids, block_docs, order, queries, grads, swapped, stat_own, docs, early, tail, *refs,
                heads, head_size, half_rows):
    dq_own, dq_out, pack_out, rest_out = refs[:4]
    lse_doc, dq_acc, dq_oth, pack, rest, q_all, g_all, terms, stats, k_grp, v_grp, kt_grp, dk_acc, dv_acc, sems = refs[4:]
    blocks = block_docs.shape[0]
    cols = early.shape[0]
    tok = docs.shape[1]
    part = half_rows // cols
    scaling = head_size ** (-0.5)
    log2e = math.log2(math.e)
    first, count = order[blocks], order[blocks + 1]
    loads = [pltpu.make_async_copy(swapped.at[2 * tok:, :], terms, sems.at[0])]
    for h in range(heads):
        span = slice(h * head_size, (h + 1) * head_size)
        loads += [
            pltpu.make_async_copy(queries.at[:, span], q_all.at[h], sems.at[1 + h]),
            pltpu.make_async_copy(grads.at[:, span], g_all.at[h], sems.at[1 + heads + h]),
            pltpu.make_async_copy(swapped.at[:tok, span], q_all.at[heads + h], sems.at[1 + 2 * heads + h]),
            pltpu.make_async_copy(swapped.at[tok:2 * tok, span], g_all.at[heads + h], sems.at[1 + 3 * heads + h]),
        ]
    for load in loads:
        load.start()

    loads[0].wait()
    theirs = jnp.zeros((2 * heads, tok), jnp.float32)
    for t in range(TERMS - 1, -1, -1):
        theirs = theirs + terms[t * 2 * heads:(t + 1) * 2 * heads, :].astype(jnp.float32)
    stats[:heads, :] = stat_own[:heads, :]
    stats[heads:, :] = theirs[:heads]
    lse_all = jnp.concatenate([stat_own[heads:, :], theirs[heads:]], axis=0) * log2e
    doc_row = docs[...]
    for d in range(DOC_SLOTS):
        lse_doc[d] = jnp.where(doc_row == d, lse_all, MASKED)
    dq_own[...] = jnp.zeros_like(dq_own)
    dq_acc[...] = jnp.zeros_like(dq_acc)
    pack[...] = jnp.zeros_like(pack)

    @pl.when(count > SLOTS)
    def _():
        rest[...] = jnp.zeros_like(rest)

    for load in loads[1:]:
        load.wait()

    def group_step(grp, carry):
        base = grp * GROUP
        group_docs = []
        for s in range(GROUP):
            b = order[first + jnp.minimum(base + s, count - 1)]
            group_docs.append(block_docs[b])

        def get(ref, slot):
            for s in range(GROUP):
                for j in range(cols):
                    rows = slice(s * half_rows + j * part, s * half_rows + (j + 1) * part)
                    k_grp[rows, :] = ref[j, slot + s, :, :head_size]
                    v_grp[rows, :] = ref[j, slot + s, :, head_size:]

        @pl.when(base < SLOTS)
        def _():
            get(early, jnp.minimum(base, SLOTS - GROUP))

        @pl.when(base >= SLOTS)
        def _():
            get(tail, jnp.maximum(base - SLOTS, 0))

        slot_docs = [jnp.where(base + s < count, group_docs[s], PAD_DOC) for s in range(GROUP)]
        kt_grp[...] = k_grp[...].T
        dk_acc[...] = jnp.zeros_like(dk_acc)
        dv_acc[...] = jnp.zeros_like(dv_acc)
        wanted = [
            (group_docs[0] <= doc_ids[start + CHUNK - 1]) & (group_docs[-1] >= doc_ids[start])
            for start in range(0, tok, CHUNK)
        ]

        def work(toks):
            for h in range(2 * heads):
                query = q_all[h, toks, :]
                grad = g_all[h, toks, :]
                delta = stats[h:h + 1, toks]
                score = dot_nt(k_grp[...], query)
                dprob = dot_nt(v_grp[...], grad)
                prob_low, dscore = [], []
                for s in range(GROUP):
                    rows = slice(s * half_rows, (s + 1) * half_rows)
                    shift = lse_doc[slot_docs[s], h:h + 1, toks]
                    prob = jnp.exp2(score[rows] * (scaling * log2e) - shift)
                    prob_low.append(prob.astype(jnp.bfloat16))
                    dscore.append((prob * (dprob[rows] - delta) * scaling).astype(jnp.bfloat16))
                low, ds = jnp.concatenate(prob_low, axis=0), jnp.concatenate(dscore, axis=0)
                dk_acc[...] += dot_nn(ds, query)
                dv_acc[...] += dot_nn(low, grad)
                turned = dot_nn(kt_grp[...], ds)
                if h < heads:
                    dq_own[h, :, toks] += turned
                else:
                    dq_acc[h - heads, :, toks] += turned

        @pl.when(wanted[0] & wanted[1])
        def _():
            work(slice(0, tok))

        for i, other in ((0, 1), (1, 0)):

            @pl.when(wanted[i] & jnp.logical_not(wanted[other]))
            def _():
                work(slice(i * CHUNK, (i + 1) * CHUNK))

        def put(out, slot):
            for s in range(GROUP):
                for j in range(cols):
                    rows = slice(s * half_rows + j * part, s * half_rows + (j + 1) * part)
                    out[j, slot + s, :, :head_size] = dk_acc[rows, :].astype(jnp.bfloat16)
                    out[j, slot + s, :, head_size:] = dv_acc[rows, :].astype(jnp.bfloat16)

        @pl.when(base < SLOTS)
        def _():
            put(pack, jnp.minimum(base, SLOTS - GROUP))

        @pl.when(base >= SLOTS)
        def _():
            put(rest, jnp.maximum(base - SLOTS, 0))

        return carry

    lax.fori_loop(0, (count + GROUP - 1) // GROUP, group_step, 0)
    for h in range(heads):
        dq_oth[h] = dq_acc[h].astype(jnp.bfloat16)
    stores = [
        pltpu.make_async_copy(pack, pack_out, sems.at[0]),
        pltpu.make_async_copy(dq_oth, dq_out, sems.at[1]),
    ]
    for store in stores:
        store.start()
    late = pltpu.make_async_copy(rest, rest_out, sems.at[2])

    @pl.when(count > SLOTS)
    def _():
        late.start()
        late.wait()

    for store in stores:
        store.wait()


def local_grads(doc_ids, block_docs, order, queries, grads, swapped, stat_own, early, tail, half_rows,
                interpret=False):
    tok, width = queries.shape
    cols = early.shape[0]
    head_size = early.shape[3] // 2
    blocks = block_docs.shape[0]
    heads = width // head_size
    smem = pl.BlockSpec(memory_space=pltpu.SMEM)
    vmem = pl.BlockSpec(memory_space=pltpu.VMEM)
    hbm = pl.BlockSpec(memory_space=pltpu.HBM)
    rows = GROUP * half_rows
    turned = (heads, head_size, tok)
    pack = (cols, SLOTS, half_rows // cols, 2 * head_size)
    rest = (cols, blocks - SLOTS, half_rows // cols, 2 * head_size)
    return pl.pallas_call(
        functools.partial(grad_kernel, heads=heads, head_size=head_size, half_rows=half_rows),
        in_specs=[smem] * 3 + [hbm] * 2 + [pl.BlockSpec(memory_space=pl.ANY)] + [vmem] * 4,
        out_specs=[vmem] + [hbm] * 3,
        out_shape=[
            jax.ShapeDtypeStruct(turned, jnp.float32),
            pltpu.HBM(turned, jnp.bfloat16),
            pltpu.HBM(pack, jnp.bfloat16),
            pltpu.HBM(rest, jnp.bfloat16),
        ],
        scratch_shapes=[
            pltpu.VMEM((DOC_SLOTS, 2 * heads, tok), jnp.float32),
            pltpu.VMEM(turned, jnp.float32),
            pltpu.VMEM(turned, jnp.bfloat16),
            pltpu.VMEM(pack, jnp.bfloat16),
            pltpu.VMEM(rest, jnp.bfloat16),
            pltpu.VMEM((2 * heads, tok, head_size), jnp.bfloat16),
            pltpu.VMEM((2 * heads, tok, head_size), jnp.bfloat16),
            pltpu.VMEM((TERM_ROWS, tok), jnp.bfloat16),
            pltpu.VMEM((2 * heads, tok), jnp.float32),
            pltpu.VMEM((rows, head_size), jnp.bfloat16),
            pltpu.VMEM((rows, head_size), jnp.bfloat16),
            pltpu.VMEM((head_size, rows), jnp.bfloat16),
            pltpu.VMEM((rows, head_size), jnp.float32),
            pltpu.VMEM((rows, head_size), jnp.float32),
            pltpu.SemaphoreType.DMA((1 + 4 * heads,)),
        ],
        compiler_params=pltpu.CompilerParams(vmem_limit_bytes=32 << 20),
        interpret=interpret,
    )(doc_ids, block_docs, order, *in_hbm(queries, grads), swapped, stat_own, doc_ids[None, :], early, tail)


def spread_kernel(table, near, *refs, blocks):
    pieces, out = refs[:-1], refs[-1]
    cols = pieces[0].shape[0]

    def step(b, carry):
        total = jnp.zeros(out.shape[1:], jnp.float32)
        for i in range(cols):
            slot = table[b] - near[i]
            begin = 0
            for piece in pieces:
                size = piece.shape[1]
                here = (slot >= begin) & (slot < jnp.minimum(near[cols + i], begin + size))
                part = piece[i, jnp.clip(slot - begin, 0, size - 1)].astype(jnp.float32)
                total = total + jnp.where(here, part, 0.0)
                begin += size
        out[b] = total.astype(jnp.bfloat16)
        return carry

    lax.fori_loop(0, blocks, step, 0, unroll=4)


def spread(table, near, pieces, blocks, interpret=False):
    smem = pl.BlockSpec(memory_space=pltpu.SMEM)
    vmem = pl.BlockSpec(memory_space=pltpu.VMEM)
    return pl.pallas_call(
        functools.partial(spread_kernel, blocks=blocks),
        in_specs=[smem] * 2 + [vmem] * len(pieces),
        out_specs=vmem,
        out_shape=jax.ShapeDtypeStruct((blocks,) + pieces[0].shape[2:], jnp.bfloat16),
        compiler_params=pltpu.CompilerParams(vmem_limit_bytes=12 << 20),
        interpret=interpret,
    )(table, near, *pieces)


def body(queries, keys, values, outputs, out_grad, lse, doc_ids, image_docs):
    cores = lax.axis_size("c")
    cols = lax.axis_size("yl")
    planes = lax.axis_size("z")
    owners = lax.axis_size("x") * lax.axis_size("yh")
    tok = queries.shape[0]
    heads = lse.shape[1]
    head_size = queries.shape[1] // heads
    blocks = image_docs.shape[0]
    half_rows = keys.shape[0] // cores
    piece = half_rows // (owners * cols)
    swap = [(i, cores - 1 - i) for i in range(cores)]

    where = jnp.stack([lax.axis_index("c"), lax.axis_index(("x", "yh"))]).astype(jnp.int32)
    both, stat_own, swap_out, table, order = ready(
        doc_ids, image_docs, where, keys, values, queries, outputs, out_grad, lse.T, owners, cores, cols
    )
    swapped = lax.ppermute(swap_out, "c", swap)

    shares = lax.all_to_all(both, "yl", 0, 0, tiled=True)
    column = lax.all_gather(join(shares), "z", axis=0, tiled=True)
    plane = lax.axis_index("z").astype(jnp.int32).reshape(1)
    wanted, late, near = choose(order, plane, column, planes, cols, blocks)
    early = lax.all_to_all(wanted, "yl", 0, 0, tiled=True)
    tail = lax.cond(
        near[2 * cols] <= SLOTS, jnp.zeros_like, lambda a: lax.all_to_all(a, "yl", 0, 0, tiled=True), late
    )
    dq_own, dq_oth, pack, rest = local_grads(
        doc_ids, image_docs, order, queries, out_grad, swapped, stat_own, early, tail, half_rows
    )
    dq_back = lax.ppermute(dq_oth, "c", swap)

    shared = lax.all_to_all(pack, "yl", 0, 0, tiled=True)

    def some(pieces):
        return spread(table, near, pieces[:1], blocks)

    def every(pieces):
        late = lax.all_to_all(pieces[1], "yl", 0, 0, tiled=True)
        return spread(table, near, (pieces[0], late), blocks)

    sums = lax.cond(near[2 * cols] <= SLOTS, some, every, (shared, rest))
    parts = lax.all_to_all(sums.reshape(planes, half_rows, 2 * head_size), "z", 0, 0, tiled=True)
    home = jnp.sum(parts.astype(jnp.float32), axis=0).astype(jnp.bfloat16)
    shares = lax.all_to_all(home.reshape(cols * owners, piece, 2 * head_size), ("yl", "x", "yh"), 0, 0, tiled=True)
    kv_grad = jnp.transpose(shares.reshape(cols, owners, piece, 2 * head_size), (0, 2, 1, 3)).reshape(
        cols * piece, owners * 2 * head_size
    )
    dquery = (dq_own + dq_back.astype(jnp.float32)).astype(jnp.bfloat16)
    query_grad = jnp.transpose(dquery, (2, 0, 1)).reshape(tok, heads * head_size)
    return (query_grad, kv_grad)


def solution(mesh):
    torus = Mesh(mesh.devices.reshape(12, 4, 4, 2, 2), BLK + PATCH)
    placed = (
        P(BLK, PATCH),
        P(BLK, None),
        P(BLK, None),
        P(BLK, PATCH),
        P(BLK, PATCH),
        P(BLK, PATCH),
        P(BLK),
        P(),
    )
    return jax.shard_map(
        body,
        mesh=torus,
        in_specs=placed,
        out_specs=(P(BLK, PATCH), P(BLK + PATCH, None)),
        check_vma=False,
    )
```
